512 devices in a mesh: tile: 32 (over y, z_lo), pos: 16 (over x, z_hi, core).
Axes of the slice: x: 4, y: 8, z: 8 (z_hi: 2, z_lo: 4; z = z_hi * 4 + z_lo), core: 2. Of those that a mesh axis runs over, the one named last changes fastest.
Arguments:
- amplitude: float32 [32, 2, 256, 256], P('tile'), may hold values from 0.6 to 1
- phase_map: float32 [32, 2, 256, 256], P('tile'), may hold values from -3.140625 to 3.140625
- probe_modes: float32 [2, 3, 128, 128], replicated, may hold values from -4 to 4
- offsets: int32 [32, 32, 2], P('tile', 'pos'), may hold values from 0 to 128
- pos_counts: int32 [32, 16], P('tile', 'pos'), may hold values from 1 to 2, as said below
- measured: float32 [32, 32, 128, 128], P('tile', 'pos'), may hold values from 0.1 to 2
Outputs:
- updated_object: float32 [32, 2, 2, 256, 256], P('tile')
The draws below stay inside these ranges and needn't reach their ends.
Inputs may be any that keep to these rules, and one draw needn't show every extreme that they name: The first pos_counts[t, p] slots of subset p of tile t hold positions; its other slots are padding and take no part. In every tile some subset has 2 live slots.
All inputs are finite; a program needn't handle non-finite values.
Results may differ from the reference program's by a relative error of at most 0.0015.
Values sent between devices are 32-bit elements; how exact they have to be, the bound alone decides.
A program may use at most 64 MiB of HBM per device.

```python
import math
import jax
import jax.numpy as jnp
from jax import lax

TILE = 256
CORRELATION = 64
WIN = 128
MODES = 3
SLICES = 2
ITERS = 1
GRID_COLS = 4
P_DEV = 2
TILES = 32
SUBSETS = 16
SLOTS = 32


def draw_pos_counts(key, part):
    key_spread = jax.random.fold_in(key, 11)
    key_peak = jax.random.fold_in(key, 23)
    light_most = max(1, (P_DEV + 1) // 2)
    spread_counts = jax.random.randint(key_spread, (TILES, SUBSETS), 1, light_most + 1)
    busiest = jax.random.randint(key_peak, (TILES, 1), 0, SUBSETS)
    is_busiest = jnp.arange(SUBSETS)[None, :] == busiest
    return jnp.where(is_busiest, P_DEV, spread_counts).astype(jnp.int32)


def set_ends(entries, rng, smallest, high):
    longest = entries.shape.index(max(entries.shape))
    spots = []
    for shift in (0, 1):
        where = [jax.random.randint(jax.random.fold_in(rng, axis), (), 0, length) for axis, length in enumerate(entries.shape)]
        where[longest] = (where[longest] + shift) % entries.shape[longest]
        spots.append(tuple(where))
    return entries.at[spots[0]].set(smallest).at[spots[1]].set(high)


def block_levels(own_key, shape, split, smallest, top_value):
    loudness, own = 1.0, jax.random.fold_in(own_key, 6)
    for position, parts in split:
        heights = jnp.exp(jax.random.uniform(jax.random.fold_in(own, position), (parts,), jnp.float32, smallest / len(split), top_value / len(split)))
        loudness = loudness * jnp.repeat(heights, shape[position] // parts).reshape([-1 if axis == position else 1 for axis in range(len(shape))])
    return loudness


def gaussian(own_key, shape, spread, reach, kind=jnp.bfloat16):
    drawn = jax.random.normal(own_key, shape, jnp.float32) * spread
    return jnp.minimum(jnp.maximum(drawn, -reach), reach).astype(kind)


def setup_inputs(seed: int = 0) -> dict:
    arg_keys = jax.random.split(jax.random.key(seed), 7)
    return {
        "amplitude": jnp.clip(0.6 + 0.39999998 * jax.random.uniform(arg_keys[0], (TILES, SLICES, TILE, TILE), jnp.float32) ** block_levels(arg_keys[0], (TILES, SLICES, TILE, TILE), ((0, 32),), -0.2, 0.2), 0.6, 1.0),
        "phase_map": jnp.clip(jax.random.uniform(arg_keys[1], (TILES, SLICES, TILE, TILE), jnp.float32, -3.140625, 3.140625), -3.140625, 3.140625),
        "probe_modes": gaussian(arg_keys[2], (2, MODES, WIN, WIN), 0.3, 4.0, jnp.float32),
        "offsets": set_ends(jax.random.randint(arg_keys[3], (TILES, SLOTS, 2), 0, TILE - WIN + 1), jax.random.fold_in(arg_keys[3], 1), 0, TILE - WIN).astype(jnp.int32),
        "pos_counts": draw_pos_counts(jax.random.fold_in(arg_keys[6], 71), 0),
        "measured": jnp.clip(jnp.exp(math.log(2.0) - 2.9957323 * jax.random.uniform(arg_keys[5], (TILES, SLOTS, WIN, WIN), jnp.float32) ** block_levels(arg_keys[5], (TILES, SLOTS, WIN, WIN), ((0, 32), (1, 16)), -0.2, 0.2)), 0.1, 2.0),
    }


step_size = 0.1
fresnel_rate = 0.0123

def make_tables(extent):
    counter = jnp.arange(extent, dtype=jnp.int32)
    product = counter[:, None] * counter[None, :] % extent
    angles = product.astype(jnp.float32) * (2.0 * math.pi / extent)
    scaling = 1.0 / math.sqrt(extent)
    table_re = (jnp.cos(angles) * scaling).astype(jnp.bfloat16)
    table_im = (-jnp.sin(angles) * scaling).astype(jnp.bfloat16)
    centered = ((counter + extent // 2) % extent - extent // 2).astype(jnp.float32)
    phases = -fresnel_rate * (centered[:, None] * centered[:, None] + centered[None, :] * centered[None, :])
    return (table_re, table_im, jnp.cos(phases), jnp.sin(phases))

def right_pass(wave_re, wave_im, table_re, table_im):
    extent = wave_re.shape[-1]
    stacked = jnp.concatenate([wave_re, wave_im], axis=0).astype(jnp.bfloat16).reshape(-1, extent)
    joined = jnp.concatenate([table_re, table_im], axis=1)
    result = jnp.dot(stacked, joined, preferred_element_type=jnp.float32)
    half_rows = result.shape[0] // 2
    upper_part = result[:half_rows]
    lower_part = result[half_rows:]
    out_re = upper_part[:, :extent] - lower_part[:, extent:]
    out_im = upper_part[:, extent:] + lower_part[:, :extent]
    return (out_re.reshape(wave_re.shape), out_im.reshape(wave_re.shape))

def transform(wave_re, wave_im, table_re, table_im):
    first_re, first_im = right_pass(wave_re, wave_im, table_re, table_im)
    second_re, second_im = right_pass(jnp.swapaxes(first_re, 1, 2), jnp.swapaxes(first_im, 1, 2), table_re, table_im)
    return (jnp.swapaxes(second_re, 1, 2), jnp.swapaxes(second_im, 1, 2))

def slot_loss(cropped, probe_modes, target, tables):
    table_re, table_im, kernel_re, kernel_im = tables
    layers = cropped.shape[1]
    wave_re = probe_modes[0] * cropped[0, 0] - probe_modes[1] * cropped[1, 0]
    wave_im = probe_modes[0] * cropped[1, 0] + probe_modes[1] * cropped[0, 0]
    for slice_index in range(1, layers):
        spread_re, spread_im = transform(wave_re, wave_im, table_re, table_im)
        moved_re = spread_re * kernel_re - spread_im * kernel_im
        moved_im = spread_re * kernel_im + spread_im * kernel_re
        inverse_re, inverse_im = transform(moved_re, moved_im, table_re, -table_im)
        wave_re = inverse_re * cropped[0, slice_index] - inverse_im * cropped[1, slice_index]
        wave_im = inverse_re * cropped[1, slice_index] + inverse_im * cropped[0, slice_index]
    far_re, far_im = transform(wave_re, wave_im, table_re, table_im)
    intensity = lax.optimization_barrier(jnp.sum(far_re * far_re + far_im * far_im, axis=0))
    misfit = intensity - target
    return 0.5 * jnp.sum(misfit * misfit)

def slot_gradient(cropped, probe_modes, target, tables):
    return jax.grad(slot_loss)(cropped, probe_modes, target, tables)

def tile_gradient(tile_object, probe_modes, tile_offsets, tile_live, tile_target, tables):
    window = tile_target.shape[-1]
    layers = tile_object.shape[1]
    anchor = jnp.zeros((), jnp.int32)

    def visit_slot(accumulated, slot_entry):
        offset_pair, is_live, target = slot_entry
        starts = (anchor, anchor, offset_pair[0].astype(jnp.int32), offset_pair[1].astype(jnp.int32))

        def compute_slot(current):
            cropped = lax.dynamic_slice(tile_object, starts, (2, layers, window, window))
            gradient = slot_gradient(cropped, probe_modes, target, tables)
            region = lax.dynamic_slice(current, starts, (2, layers, window, window))
            return lax.dynamic_update_slice(current, region + gradient, starts)

        def keep_total(current):
            return current
        return (lax.cond(is_live, compute_slot, keep_total, accumulated), None)
    accumulated, unused = lax.scan(visit_slot, jnp.zeros_like(tile_object), (tile_offsets, tile_live, tile_target))
    return accumulated

def add_strips(gradients):
    extent = gradients.shape[-1]
    row_count = gradients.shape[-2]
    zero_tiles = jnp.zeros_like(gradients[:GRID_COLS])
    from_left = jnp.concatenate([zero_tiles[:1], gradients[:-1]], axis=0)[..., extent - CORRELATION:]
    from_right = jnp.concatenate([gradients[1:], zero_tiles[:1]], axis=0)[..., :CORRELATION]
    from_above = jnp.concatenate([zero_tiles, gradients[:-GRID_COLS]], axis=0)[..., row_count - CORRELATION:, :]
    from_below = jnp.concatenate([gradients[GRID_COLS:], zero_tiles], axis=0)[..., :CORRELATION, :]
    result = gradients.at[..., :CORRELATION].add(from_left)
    result = result.at[..., extent - CORRELATION:].add(from_right)
    result = result.at[..., :CORRELATION, :].add(from_above)
    result = result.at[..., row_count - CORRELATION:, :].add(from_below)
    return result

def reference(amplitude, phase_map, probe_modes, offsets, pos_counts, measured):
    tables = make_tables(WIN)
    current = jnp.stack([amplitude * jnp.cos(phase_map), amplitude * jnp.sin(phase_map)], axis=1)
    slot_index = jnp.arange(SLOTS, dtype=jnp.int32)
    live_slots = slot_index[None, :] % P_DEV < jnp.repeat(pos_counts, P_DEV, axis=1)

    def per_tile(tile_entry):
        tile_object, tile_offsets, tile_live, tile_target = tile_entry
        return tile_gradient(tile_object, probe_modes, tile_offsets, tile_live, tile_target, tables)
    for sweep_index in range(ITERS):
        gradients = lax.map(per_tile, (current, offsets, live_slots, measured))
        current = current - step_size * add_strips(gradients)
    return current
```

```python
import functools
import math

import jax
import jax.numpy as jnp
import numpy as np
from jax import lax
from jax.experimental import pallas as pl
from jax.experimental.pallas import tpu as pltpu
from jax.sharding import PartitionSpec as P

MESH = pl.DeviceIdType.MESH
TILE = 256
WIN = 128
EDGE = 64
MODES = 3
LAYERS = 2
SLOTS = 2
SPAN = WIN + 8
STEP = 0.1
FRESNEL = 0.0123
SIN = (0.9999999957326958, -0.16666657991741893, 0.008333051059307331, -0.0001980907498047039, 2.605224199925007e-06)
COS = (0.9999999997806426, -0.49999999358456015, 0.04166663625748454, -0.001388836139270363, 2.476016095941152e-05, -2.6051488147238807e-07)


def make_tables():
    counter = np.arange(WIN)
    angles = (np.outer(counter, counter) % WIN).astype(np.float32) * np.float32(2.0 * math.pi / WIN)
    scaling = np.float32(1.0 / math.sqrt(WIN))
    f_re = (np.cos(angles) * scaling).astype(jnp.bfloat16)
    f_im = (-np.sin(angles) * scaling).astype(jnp.bfloat16)
    forward = np.block([[f_re, f_im], [-f_im, f_re]])
    inverse = np.block([[f_re, -f_im], [f_im, f_re]])
    centered = ((counter + WIN // 2) % WIN - WIN // 2).astype(np.float32)
    square = centered * centered
    phases = np.float32(-FRESNEL) * (square[:, None] + square[None, :])
    kernel = np.stack([np.cos(phases), np.sin(phases)]).astype(np.float32)
    return np.stack([forward, inverse]).astype(jnp.bfloat16), kernel


def horner(terms, u):
    total = jnp.full_like(u, terms[-1])
    for term in terms[-2::-1]:
        total = total * u + term
    return total


def polar(amplitude, phase):
    half = phase * 0.5
    u = half * half
    sine = half * horner(SIN, u)
    cosine = horner(COS, u)
    return amplitude - (2.0 * amplitude) * (sine * sine), (2.0 * amplitude) * (sine * cosine)


def times(a, b):
    return a[0] * b[0] - a[1] * b[1], a[0] * b[1] + a[1] * b[0]


def times_conj(a, b):
    return a[0] * b[0] + a[1] * b[1], a[1] * b[0] - a[0] * b[1]


def right_pass(waves, table):
    rows = [jnp.concatenate([re.astype(jnp.bfloat16), im.astype(jnp.bfloat16)], axis=1) for re, im in waves]
    result = jnp.dot(jnp.concatenate(rows, axis=0), table, preferred_element_type=jnp.float32)
    return [(result[i * WIN : (i + 1) * WIN, :WIN], result[i * WIN : (i + 1) * WIN, WIN:]) for i in range(len(waves))]


def left_pass(waves, table):
    columns = [jnp.concatenate([re.astype(jnp.bfloat16), im.astype(jnp.bfloat16)], axis=0) for re, im in waves]
    result = jnp.dot(table, jnp.concatenate(columns, axis=1), preferred_element_type=jnp.float32)
    return [(result[:WIN, i * WIN : (i + 1) * WIN], result[WIN:, i * WIN : (i + 1) * WIN]) for i in range(len(waves))]


def transform(waves, right, left):
    return left_pass(right_pass(waves, right), left)


def transform_back(waves, right, left):
    return right_pass(left_pass(waves, left), right)


def crop(ref, layer, base, shift, column):
    rows = ref[layer, pl.ds(base, SPAN), :]
    rows = pltpu.roll(rows, lax.rem(TILE - column, TILE), 1)[:, :WIN]
    return pltpu.roll(rows, lax.rem(SPAN - shift, SPAN), 0)[:WIN]


def spread_out(value, shift, column):
    tall = jnp.concatenate([value, jnp.zeros((SPAN - WIN, WIN), value.dtype)], axis=0)
    tall = pltpu.roll(tall, shift, 0)
    return pltpu.roll(jnp.concatenate([tall, jnp.zeros_like(tall)], axis=1), column, 1)


def add_all(values):
    total = values[0]
    for value in values[1:]:
        total = total + value
    return total


def slot_gradient(layers, probe_ref, target, tables_ref, kernel_ref):
    forward, inverse = tables_ref[0], tables_ref[1]
    kernel = (kernel_ref[0], kernel_ref[1])
    probes = [(probe_ref[0, m], probe_ref[1, m]) for m in range(MODES)]
    waves = [times(probe, layers[0]) for probe in probes]
    spread = transform(waves, forward, inverse)
    moved = [times(wave, kernel) for wave in spread]
    returned = transform(moved, inverse, forward)
    waves = [times(wave, layers[1]) for wave in returned]
    far = transform(waves, forward, inverse)
    misfit = add_all([re * re + im * im for re, im in far]) - target
    twice = misfit + misfit
    grads = transform_back([(twice * re, twice * im) for re, im in far], inverse, forward)
    second = [times_conj(grad, wave) for grad, wave in zip(grads, returned)]
    second = (add_all([v[0] for v in second]), add_all([v[1] for v in second]))
    grads = transform_back([times_conj(grad, layers[1]) for grad in grads], forward, inverse)
    grads = transform_back([times_conj(grad, kernel) for grad in grads], inverse, forward)
    first = [times_conj(grad, probe) for grad, probe in zip(grads, probes)]
    first = (add_all([v[0] for v in first]), add_all([v[1] for v in first]))
    return first, second


def gradient_kernel(off_ref, count_ref, amp_ref, phase_ref, probe_ref, measured_ref, tables_ref, kernel_ref, out_ref):
    out_ref[...] = jnp.zeros_like(out_ref)
    for slot in range(SLOTS):
        row, column = off_ref[slot, 0], off_ref[slot, 1]
        base = pl.multiple_of(jnp.minimum(row // 8 * 8, TILE - SPAN), 8)
        shift = row - base
        live = slot < count_ref[0, 0]
        layers = [
            polar(crop(amp_ref, layer, base, shift, column), crop(phase_ref, layer, base, shift, column))
            for layer in range(LAYERS)
        ]
        grads = slot_gradient(layers, probe_ref, measured_ref[slot], tables_ref, kernel_ref)
        for layer in range(LAYERS):
            for part in range(2):
                value = jnp.where(live, grads[layer][part], 0.0)
                out_ref[2 * part + layer, pl.ds(base, SPAN), :] += spread_out(value, shift, column)


def combine_kernel(
    part_ref, amp_ref, phase_ref, out_ref,
    pair, half, relay, merged, direct, final, block, zin, strips, strips_in, rows_in, send, recv,
):
    tile, pos = lax.axis_index("tile"), lax.axis_index("pos")
    tiles = lax.axis_size("tile")
    core, z_hi, x = lax.rem(pos, 2), lax.rem(pos // 2, 2), pos // 4
    z_lo = lax.rem(tile, 4)
    xo, xp, xm = lax.rem(x + 2, 4), lax.rem(x + 1, 4), lax.rem(x + 3, 4)

    def place(x_, z_, core_):
        return x_ * 4 + z_ * 2 + core_

    here = tile
    sibling = {"tile": here, "pos": place(x, z_hi, 1 - core)}
    right_x = {"tile": here, "pos": place(xp, z_hi, core)}
    left_x = {"tile": here, "pos": place(xm, z_hi, core)}
    across = {"tile": here, "pos": place(x, 1 - z_hi, core)}
    after_z = jnp.where(z_lo == 3, 1 - z_hi, z_hi)
    before_z = jnp.where(z_lo == 0, 1 - z_hi, z_hi)
    after = {"tile": lax.rem(tile + 1, tiles), "pos": place(x, after_z, core)}
    before = {"tile": lax.rem(tile + tiles - 1, tiles), "pos": place(x, before_z, core)}
    vertical = {"tile": lax.rem(tile + tiles + jnp.where(core == 0, -4, 4), tiles), "pos": place(x, z_hi, 1 - core)}

    partners = (sibling, right_x, left_x, across, after, before, vertical)
    barrier = pltpu.get_barrier_semaphore()
    for partner in partners:
        pl.semaphore_signal(barrier, inc=1, device_id=partner, device_id_type=MESH)
    pl.semaphore_wait(barrier, len(partners))

    started = []

    def push(index, src, dst, device):
        copy = pltpu.make_async_remote_copy(
            src_ref=src, dst_ref=dst, send_sem=send.at[index], recv_sem=recv.at[index],
            device_id=device, device_id_type=MESH,
        )
        copy.start()
        started.append(copy)
        return copy

    mine = pl.ds(pl.multiple_of(core * WIN, WIN), WIN)
    other = pl.ds(pl.multiple_of((1 - core) * WIN, WIN), WIN)
    upper, lower = pl.ds(0, EDGE), pl.ds(EDGE, EDGE)

    order = (xo, xp, xm, x)
    swaps = [push(k, part_ref.at[order[k], other], pair.at[k], sibling) for k in range(4)]

    def reduce_pair(k):
        swaps[k].wait_recv()
        half[k] = part_ref[order[k], mine, :] + pair[k]

    reduce_pair(0)
    to_right = push(4, half.at[0, upper], relay.at[0], right_x)
    to_left = push(5, half.at[0, lower], relay.at[1], left_x)
    reduce_pair(1)
    direct_right = push(6, half.at[1, lower], direct.at[1], right_x)
    reduce_pair(2)
    direct_left = push(7, half.at[2, upper], direct.at[0], left_x)
    reduce_pair(3)
    to_right.wait_recv()
    merged[0] = relay[0] + half[1, 0:EDGE, :]
    last_right = push(8, merged.at[0], final.at[0], right_x)
    to_left.wait_recv()
    merged[1] = relay[1] + half[2, EDGE:WIN, :]
    last_left = push(9, merged.at[1], final.at[1], left_x)
    direct_left.wait_recv()
    last_right.wait_recv()
    block[0:EDGE, :] = half[3, 0:EDGE, :] + (direct[0] + final[0])
    direct_right.wait_recv()
    last_left.wait_recv()
    block[EDGE:WIN, :] = half[3, EDGE:WIN, :] + (direct[1] + final[1])

    swap_z = push(10, block, zin, across)
    swap_z.wait()
    block[...] = block[...] + zin[...]

    edge_rows = pl.ds(pl.multiple_of(core * EDGE, EDGE), EDGE)
    swap_rows = push(11, block.at[edge_rows], rows_in, vertical)
    lane = lax.broadcasted_iota(jnp.int32, (EDGE, WIN), 1)
    low = lane < EDGE
    strips[0] = jnp.where(low, pltpu.roll(block[0:EDGE, WIN:], EDGE, 1), block[EDGE:WIN, WIN:])
    strips[1] = jnp.where(low, block[0:EDGE, :WIN], pltpu.roll(block[EDGE:WIN, :WIN], EDGE, 1))
    swap_after = push(12, strips.at[0], strips_in.at[0], after)
    swap_before = push(13, strips.at[1], strips_in.at[1], before)

    layer, part = lax.rem(x, 2), x // 2
    base = polar(amp_ref[layer, mine, :], phase_ref[layer, mine, :])
    base = jnp.where(part == 0, base[0], base[1])

    swap_after.wait_recv()
    swap_before.wait_recv()
    from_left = jnp.where(tile > 0, strips_in[0], 0.0)
    from_right = jnp.where(tile < tiles - 1, strips_in[1], 0.0)
    left_top = jnp.where(low, from_left, 0.0)
    left_bottom = jnp.where(low, pltpu.roll(from_left, EDGE, 1), 0.0)
    right_top = jnp.where(low, 0.0, pltpu.roll(from_right, EDGE, 1))
    right_bottom = jnp.where(low, 0.0, from_right)
    sides = jnp.concatenate(
        [jnp.concatenate([left_top, right_top], axis=1), jnp.concatenate([left_bottom, right_bottom], axis=1)], axis=0
    )
    swap_rows.wait_recv()
    vertical_live = jnp.where(core == 0, tile >= 4, tile < tiles - 4)
    edge = jnp.where(vertical_live, rows_in[...], 0.0)
    top = jnp.where(core == 0, edge, 0.0)
    bottom = jnp.where(core == 0, 0.0, edge)
    combined = block[...] + sides + jnp.concatenate([top, bottom], axis=0)
    out_ref[x, mine, :] = base - STEP * combined

    top_rows = pl.ds(pl.multiple_of(core * WIN, EDGE), EDGE)
    bottom_rows = pl.ds(pl.multiple_of(core * WIN + EDGE, EDGE), EDGE)

    def share(index, plane, rows, device):
        return push(index, out_ref.at[plane, rows], out_ref.at[plane, rows], device)

    a_right = share(14, x, top_rows, right_x)
    b_left = share(15, x, bottom_rows, left_x)
    b_right = share(16, x, bottom_rows, right_x)
    a_left = share(17, x, top_rows, left_x)
    pairs = [share(18, x, mine, sibling)]
    a_right.wait_recv()
    a_next = share(19, xm, top_rows, right_x)
    b_left.wait_recv()
    b_next = share(20, xp, bottom_rows, left_x)
    b_right.wait_recv()
    pairs.append(share(21, xm, mine, sibling))
    a_left.wait_recv()
    pairs.append(share(22, xp, mine, sibling))
    a_next.wait_recv()
    b_next.wait_recv()
    pairs.append(share(23, xo, mine, sibling))
    for copy in pairs:
        copy.wait_recv()
    for copy in started:
        if copy is not swap_z:
            copy.wait_send()


def per_device(amplitude, phase_map, probe_modes, offsets, pos_counts, measured):
    tables, kernel = make_tables()
    vmem = pl.BlockSpec(memory_space=pltpu.VMEM)
    smem = pl.BlockSpec(memory_space=pltpu.SMEM)
    f32 = jnp.float32
    planes = jax.ShapeDtypeStruct((2 * LAYERS, TILE, TILE), f32)
    partial = pl.pallas_call(
        gradient_kernel,
        out_shape=planes,
        in_specs=[smem, smem] + [vmem] * 6,
        out_specs=vmem,
        name="gradient",
    )(offsets[0], pos_counts, amplitude[0], phase_map[0], probe_modes, measured[0], jnp.asarray(tables), jnp.asarray(kernel))
    updated = pl.pallas_call(
        combine_kernel,
        out_shape=planes,
        in_specs=[vmem] * 3,
        out_specs=vmem,
        scratch_shapes=[
            pltpu.VMEM((4, WIN, TILE), f32),
            pltpu.VMEM((4, WIN, TILE), f32),
            pltpu.VMEM((2, EDGE, TILE), f32),
            pltpu.VMEM((2, EDGE, TILE), f32),
            pltpu.VMEM((2, EDGE, TILE), f32),
            pltpu.VMEM((2, EDGE, TILE), f32),
            pltpu.VMEM((WIN, TILE), f32),
            pltpu.VMEM((WIN, TILE), f32),
            pltpu.VMEM((2, EDGE, WIN), f32),
            pltpu.VMEM((2, EDGE, WIN), f32),
            pltpu.VMEM((EDGE, TILE), f32),
            pltpu.SemaphoreType.DMA((24,)),
            pltpu.SemaphoreType.DMA((24,)),
        ],
        compiler_params=pltpu.CompilerParams(collective_id=0, has_side_effects=True),
        name="combine",
    )(partial, amplitude[0], phase_map[0])
    return updated.reshape(1, 2, LAYERS, TILE, TILE)


def solution(mesh):
    in_specs = (
        P("tile", None, None, None),
        P("tile", None, None, None),
        P(),
        P("tile", "pos", None),
        P("tile", "pos"),
        P("tile", "pos", None, None),
    )
    out_specs = P("tile", None, None, None, None)
    return jax.shard_map(per_device, mesh=mesh, in_specs=in_specs, out_specs=out_specs, check_vma=False)
```

```python
import functools
import math

import jax
import jax.numpy as jnp
import numpy as np
from jax import lax
from jax.experimental import pallas as pl
from jax.experimental.pallas import tpu as pltpu
from jax.sharding import PartitionSpec as P

MESH = pl.DeviceIdType.MESH
TILE = 256
WIN = 128
EDGE = 64
MODES = 3
LAYERS = 2
SLOTS = 2
STEP = 0.1
FRESNEL = 0.0123
SIN = (0.9999999957326958, -0.16666657991741893, 0.008333051059307331, -0.0001980907498047039, 2.605224199925007e-06)
COS = (0.9999999997806426, -0.49999999358456015, 0.04166663625748454, -0.001388836139270363, 2.476016095941152e-05, -2.6051488147238807e-07)


def make_tables():
    counter = np.arange(WIN)
    angles = (np.outer(counter, counter) % WIN).astype(np.float32) * np.float32(2.0 * math.pi / WIN)
    scaling = np.float32(1.0 / math.sqrt(WIN))
    f_re = (np.cos(angles) * scaling).astype(jnp.bfloat16)
    f_im = (-np.sin(angles) * scaling).astype(jnp.bfloat16)
    forward = np.block([[f_re, f_im], [-f_im, f_re]])
    inverse = np.block([[f_re, -f_im], [f_im, f_re]])
    centered = ((counter + WIN // 2) % WIN - WIN // 2).astype(np.float32)
    square = centered * centered
    phases = np.float32(-FRESNEL) * (square[:, None] + square[None, :])
    kernel = np.stack([np.cos(phases), np.sin(phases)]).astype(np.float32)
    return np.stack([forward, inverse]).astype(jnp.bfloat16), kernel


def horner(terms, u):
    total = jnp.full_like(u, terms[-1])
    for term in terms[-2::-1]:
        total = total * u + term
    return total


def polar(amplitude, phase):
    half = phase * 0.5
    u = half * half
    sine = half * horner(SIN, u)
    cosine = horner(COS, u)
    return amplitude - (2.0 * amplitude) * (sine * sine), (2.0 * amplitude) * (sine * cosine)


def times(a, b):
    return a[0] * b[0] - a[1] * b[1], a[0] * b[1] + a[1] * b[0]


def times_conj(a, b):
    return a[0] * b[0] + a[1] * b[1], a[1] * b[0] - a[0] * b[1]


def right_pass(waves, table):
    rows = [jnp.concatenate([re.astype(jnp.bfloat16), im.astype(jnp.bfloat16)], axis=1) for re, im in waves]
    result = jnp.dot(jnp.concatenate(rows, axis=0), table, preferred_element_type=jnp.float32)
    return [(result[i * WIN : (i + 1) * WIN, :WIN], result[i * WIN : (i + 1) * WIN, WIN:]) for i in range(len(waves))]


def left_pass(waves, table):
    columns = [jnp.concatenate([re.astype(jnp.bfloat16), im.astype(jnp.bfloat16)], axis=0) for re, im in waves]
    result = jnp.dot(table, jnp.concatenate(columns, axis=1), preferred_element_type=jnp.float32)
    return [(result[:WIN, i * WIN : (i + 1) * WIN], result[WIN:, i * WIN : (i + 1) * WIN]) for i in range(len(waves))]


def transform(waves, right, left):
    return left_pass(right_pass(waves, right), left)


def transform_back(waves, right, left):
    return right_pass(left_pass(waves, left), right)


def crop(ref, layer, row, column):
    rows = pltpu.roll(ref[layer], lax.rem(TILE - column, TILE), 1)[:, :WIN]
    return pltpu.roll(rows, lax.rem(TILE - row, TILE), 0)[:WIN]


def add_all(values):
    total = values[0]
    for value in values[1:]:
        total = total + value
    return total


def spread_out(value, row, column):
    wide = pltpu.roll(jnp.concatenate([value, jnp.zeros_like(value)], axis=1), column, 1)
    return pltpu.roll(jnp.concatenate([wide, jnp.zeros_like(wide)], axis=0), row, 0)


def sum_modes(pairs):
    return add_all([v[0] for v in pairs]), add_all([v[1] for v in pairs])


def fused_kernel(
    off_ref, count_ref, amp_ref, phase_ref, probe_ref, measured_ref, tables_ref, kernel_ref, out_ref,
    grad, pair, half, xin, block, zin, total, strips, strips_in, rows_in, send, recv,
):
    tile, pos = lax.axis_index("tile"), lax.axis_index("pos")
    tiles = lax.axis_size("tile")
    core, z_hi, x = lax.rem(pos, 2), lax.rem(pos // 2, 2), pos // 4
    z_lo = lax.rem(tile, 4)
    xs = [lax.rem(x + step, 4) for step in range(4)]

    def at(tile_step, x_, z_, core_):
        return {"tile": lax.rem(tile + tiles + tile_step, tiles), "pos": x_ * 4 + z_ * 2 + core_}

    sibling = at(0, x, z_hi, 1 - core)
    along_x = {step: at(0, xs[step], z_hi, core) for step in (1, 2, 3)}
    across = at(0, x, 1 - z_hi, core)
    after = at(1, x, jnp.where(z_lo == 3, 1 - z_hi, z_hi), core)
    before = at(-1, x, jnp.where(z_lo == 0, 1 - z_hi, z_hi), core)
    below = at(4, x, z_hi, core)
    above = at(-4, x, z_hi, core)

    partners = (sibling, along_x[1], along_x[3], along_x[2], across, after, before, below, above)
    barrier = pltpu.get_barrier_semaphore()
    for partner in partners:
        pl.semaphore_signal(barrier, inc=1, device_id=partner, device_id_type=MESH)

    started = []

    def push(chunk, index, src, dst, device):
        copy = pltpu.make_async_remote_copy(
            src_ref=src, dst_ref=dst, send_sem=send.at[chunk, index], recv_sem=recv.at[chunk, index],
            device_id=device, device_id_type=MESH,
        )
        copy.start()
        started.append(copy)
        return copy

    def rows_of(x_, core_):
        return pl.ds(pl.multiple_of(lax.rem(x_, 2) * 32 + core_ * 16, 16), 16)

    def flat(value):
        return value.reshape(EDGE, TILE)

    forward, inverse = tables_ref[0], tables_ref[1]
    slots = range(SLOTS)
    rows = [off_ref[slot, 0] for slot in slots]
    columns = [off_ref[slot, 1] for slot in slots]
    lives = [(count_ref[0, 0] - slot).astype(jnp.float32) for slot in slots]
    lives = [jnp.clip(jnp.full((1, TILE), live), 0.0, 1.0) for live in lives]

    def kernel():
        return kernel_ref[0], kernel_ref[1]

    def probe(m):
        return probe_ref[0, m], probe_ref[1, m]

    def collect(layer, grads):
        for part in range(2):
            parts = [spread_out(grads[slot][part], rows[slot], columns[slot]) * lives[slot] for slot in slots]
            grad[layer, part] = (parts[0] + parts[1]).reshape(4, EDGE, TILE)

    def each(stage, *lists):
        return [stage(*items) for items in zip(*lists)]

    modes = range(MODES)
    layers = []
    for slot in slots:
        layers.append(
            [
                polar(
                    crop(amp_ref, layer, rows[slot], columns[slot]),
                    crop(phase_ref, layer, rows[slot], columns[slot]),
                )
                for layer in range(LAYERS)
            ]
        )
    waves = [[times(probe(m), layers[slot][0]) for m in modes] for slot in slots]
    waves = each(lambda w: right_pass(w, forward), waves)
    waves = each(lambda w: left_pass(w, inverse), waves)
    waves = each(lambda w: [times(v, kernel()) for v in w], waves)
    waves = each(lambda w: right_pass(w, inverse), waves)
    returned = each(lambda w: left_pass(w, forward), waves)
    waves = each(lambda w, o: [times(v, o[1]) for v in w], returned, layers)
    waves = each(lambda w: right_pass(w, forward), waves)
    far = each(lambda w: left_pass(w, inverse), waves)

    def pull(slot, w):
        misfit = add_all([re * re + im * im for re, im in w]) - measured_ref[slot]
        twice = misfit + misfit
        return [(twice * re, twice * im) for re, im in w]

    waves = each(pull, slots, far)
    waves = each(lambda w: left_pass(w, forward), waves)
    waves = each(lambda w: right_pass(w, inverse), waves)
    collect(1, [sum_modes([times_conj(g, r) for g, r in zip(waves[slot], returned[slot])]) for slot in slots])

    def swap_pair(chunk):
        copies = []
        for step in (2, 1, 3, 0):
            owner = xs[step]
            src = grad.at[chunk, owner // 2, :, rows_of(owner, 1 - core)]
            copies.append((step, push(chunk, step, src, pair.at[chunk, step], sibling)))
        return copies

    def spread_x(chunk, swaps):
        copies = []
        for step, swap in swaps:
            swap.wait_recv()
            owner = xs[step]
            half[chunk, step] = grad[chunk, owner // 2, :, rows_of(owner, core), :] + pair[chunk, step]
            if step:
                copies.append(push(chunk, 3 + step, half.at[chunk, step], xin.at[chunk, step - 1], along_x[step]))
        return copies

    def swap_z(chunk, copies):
        for copy in copies:
            copy.wait_recv()
        block[chunk] = half[chunk, 0] + (xin[chunk, 0] + xin[chunk, 2] + xin[chunk, 1])
        return push(chunk, 7, block.at[chunk], zin.at[chunk], across)

    low = lax.broadcasted_iota(jnp.int32, (32, WIN), 1) < EDGE

    def swap_strips(chunk, copy):
        copy.wait_recv()
        total[chunk] = block[chunk] + zin[chunk]
        copies = [
            push(chunk, 8, total.at[chunk, 3], rows_in.at[chunk, 0], below),
            push(chunk, 9, total.at[chunk, 0], rows_in.at[chunk, 1], above),
        ]
        value = flat(total[chunk])
        left, right = value[:, :WIN], value[:, WIN:]
        strips[chunk, 0] = jnp.where(low, pltpu.roll(right[:32], EDGE, 1), right[32:])
        strips[chunk, 1] = jnp.where(low, left[:32], pltpu.roll(left[32:], EDGE, 1))
        copies.append(push(chunk, 10, strips.at[chunk, 0], strips_in.at[chunk, 0], after))
        copies.append(push(chunk, 11, strips.at[chunk, 1], strips_in.at[chunk, 1], before))
        return copies

    own_rows = rows_of(x, core)
    offset = lax.rem(x, 2) * 32 + core * 16

    def share(chunk, index, step, device):
        owner = xs[step]
        view = out_ref.at[owner // 2, chunk, :, rows_of(owner, core)]
        return push(chunk, index, view, view, device)

    def object_block(layer):
        def read(ref):
            return jnp.concatenate(
                [ref[layer, pl.ds(pl.multiple_of(p * EDGE + offset, 16), 16), :] for p in range(4)], axis=0
            )

        both = polar(read(amp_ref), read(phase_ref))
        return jnp.where(x < 2, both[0], both[1])

    def update(chunk, copies, base):
        for copy in copies:
            copy.wait_recv()
        from_left = jnp.where(tile > 0, strips_in[chunk, 0], 0.0)
        from_right = jnp.where(tile < tiles - 1, strips_in[chunk, 1], 0.0)
        left = jnp.concatenate(
            [jnp.where(low, from_left, 0.0), jnp.where(low, pltpu.roll(from_left, EDGE, 1), 0.0)], axis=0
        )
        right = jnp.concatenate(
            [jnp.where(low, 0.0, pltpu.roll(from_right, EDGE, 1)), jnp.where(low, 0.0, from_right)], axis=0
        )
        top = jnp.where(tile >= 4, rows_in[chunk, 0], 0.0)
        bottom = jnp.where(tile < tiles - 4, rows_in[chunk, 1], 0.0)
        ends = jnp.concatenate([top, jnp.zeros((32, TILE), jnp.float32), bottom], axis=0)
        combined = flat(total[chunk]) + jnp.concatenate([left, right], axis=1) + ends
        out_ref[x // 2, chunk, :, own_rows, :] = (base - STEP * combined).reshape(4, 16, TILE)
        remote = [(step, share(chunk, 11 + step, 0, along_x[step])) for step in (2, 1, 3)]
        return remote, [share(chunk, 15, 0, sibling)]

    def relay(chunk, remote, local):
        for step, copy in remote:
            copy.wait_recv()
            local.append(share(chunk, 15 + step, 4 - step, sibling))

    pl.semaphore_wait(barrier, len(partners))
    pairs_late = swap_pair(1)
    waves = each(lambda w, o: [times_conj(v, o[1]) for v in w], waves, layers)
    waves = each(lambda w: left_pass(w, inverse), waves)
    waves = each(lambda w: right_pass(w, forward), waves)
    waves = each(lambda w: [times_conj(v, kernel()) for v in w], waves)
    xs_late = spread_x(1, pairs_late)
    waves = each(lambda w: left_pass(w, forward), waves)
    waves = each(lambda w: right_pass(w, inverse), waves)
    collect(0, [sum_modes([times_conj(waves[slot][m], probe(m)) for m in modes]) for slot in slots])
    pairs_early = swap_pair(0)
    z_late = swap_z(1, xs_late)
    xs_early = spread_x(0, pairs_early)
    base_late = object_block(1)
    z_early = swap_z(0, xs_early)
    base_early = object_block(0)
    strips_late = swap_strips(1, z_late)
    strips_early = swap_strips(0, z_early)
    remote_late, local_late = update(1, strips_late, base_late)
    remote_early, local_early = update(0, strips_early, base_early)
    relay(1, remote_late, local_late)
    relay(0, remote_early, local_early)
    for copy in local_late + local_early:
        copy.wait_recv()
    for copy in started:
        copy.wait_send()


def per_device(amplitude, phase_map, probe_modes, offsets, pos_counts, measured):
    tables, kernel = make_tables()
    vmem = pl.BlockSpec(memory_space=pltpu.VMEM)
    smem = pl.BlockSpec(memory_space=pltpu.SMEM)
    f32 = jnp.float32
    updated = pl.pallas_call(
        fused_kernel,
        out_shape=jax.ShapeDtypeStruct((2, LAYERS, 4, EDGE, TILE), f32),
        in_specs=[smem, smem] + [vmem] * 6,
        out_specs=vmem,
        scratch_shapes=[
            pltpu.VMEM((LAYERS, 2, 4, EDGE, TILE), f32),
            pltpu.VMEM((LAYERS, 4, 4, 16, TILE), f32),
            pltpu.VMEM((LAYERS, 4, 4, 16, TILE), f32),
            pltpu.VMEM((LAYERS, 3, 4, 16, TILE), f32),
            pltpu.VMEM((LAYERS, 4, 16, TILE), f32),
            pltpu.VMEM((LAYERS, 4, 16, TILE), f32),
            pltpu.VMEM((LAYERS, 4, 16, TILE), f32),
            pltpu.VMEM((LAYERS, 2, 32, WIN), f32),
            pltpu.VMEM((LAYERS, 2, 32, WIN), f32),
            pltpu.VMEM((LAYERS, 2, 16, TILE), f32),
            pltpu.SemaphoreType.DMA((LAYERS, 19)),
            pltpu.SemaphoreType.DMA((LAYERS, 19)),
        ],
        compiler_params=pltpu.CompilerParams(collective_id=0, has_side_effects=True),
        name="gradient_and_combine",
    )(offsets[0], pos_counts, amplitude[0], phase_map[0], probe_modes, measured[0], jnp.asarray(tables), jnp.asarray(kernel))
    return updated.reshape(1, 2, LAYERS, TILE, TILE)


def solution(mesh):
    in_specs = (
        P("tile", None, None, None),
        P("tile", None, None, None),
        P(),
        P("tile", "pos", None),
        P("tile", "pos"),
        P("tile", "pos", None, None),
    )
    out_specs = P("tile", None, None, None, None)
    return jax.shard_map(per_device, mesh=mesh, in_specs=in_specs, out_specs=out_specs, check_vma=False)
```

```python
import functools
import math

import jax
import jax.numpy as jnp
import numpy as np
from jax import lax
from jax.experimental import pallas as pl
from jax.experimental.pallas import tpu as pltpu
from jax.sharding import PartitionSpec as P

MESH = pl.DeviceIdType.MESH
TILE = 256
WIN = 128
EDGE = 64
MODES = 3
LAYERS = 2
SLOTS = 2
SPAN = WIN + 8
LEAD = (TILE - SPAN) // 8
STEP = 0.1
FRESNEL = 0.0123
SIN = (0.9999999957326958, -0.16666657991741893, 0.008333051059307331, -0.0001980907498047039, 2.605224199925007e-06)
COS = (0.9999999997806426, -0.49999999358456015, 0.04166663625748454, -0.001388836139270363, 2.476016095941152e-05, -2.6051488147238807e-07)


def make_tables():
    counter = np.arange(WIN)
    angles = (np.outer(counter, counter) % WIN).astype(np.float32) * np.float32(2.0 * math.pi / WIN)
    scaling = np.float32(1.0 / math.sqrt(WIN))
    f_re = (np.cos(angles) * scaling).astype(jnp.bfloat16)
    f_im = (-np.sin(angles) * scaling).astype(jnp.bfloat16)
    forward = np.block([[f_re, f_im], [-f_im, f_re]])
    inverse = np.block([[f_re, -f_im], [f_im, f_re]])
    centered = ((counter + WIN // 2) % WIN - WIN // 2).astype(np.float32)
    square = centered * centered
    phases = np.float32(-FRESNEL) * (square[:, None] + square[None, :])
    kernel = np.stack([np.cos(phases), np.sin(phases)]).astype(np.float32)
    return np.stack([forward, inverse]).astype(jnp.bfloat16), kernel


def horner(terms, u):
    total = jnp.full_like(u, terms[-1])
    for term in terms[-2::-1]:
        total = total * u + term
    return total


def polar(amplitude, phase):
    half = phase * 0.5
    u = half * half
    sine = half * horner(SIN, u)
    cosine = horner(COS, u)
    return amplitude - (2.0 * amplitude) * (sine * sine), (2.0 * amplitude) * (sine * cosine)


def times(a, b):
    return a[0] * b[0] - a[1] * b[1], a[0] * b[1] + a[1] * b[0]


def times_conj(a, b):
    return a[0] * b[0] + a[1] * b[1], a[1] * b[0] - a[0] * b[1]


def right_pass(waves, table):
    rows = [jnp.concatenate([re.astype(jnp.bfloat16), im.astype(jnp.bfloat16)], axis=1) for re, im in waves]
    result = jnp.dot(jnp.concatenate(rows, axis=0), table, preferred_element_type=jnp.float32)
    return [(result[i * WIN : (i + 1) * WIN, :WIN], result[i * WIN : (i + 1) * WIN, WIN:]) for i in range(len(waves))]


def left_pass(waves, table):
    columns = [jnp.concatenate([re.astype(jnp.bfloat16), im.astype(jnp.bfloat16)], axis=0) for re, im in waves]
    result = jnp.dot(table, jnp.concatenate(columns, axis=1), preferred_element_type=jnp.float32)
    return [(result[:WIN, i * WIN : (i + 1) * WIN], result[WIN:, i * WIN : (i + 1) * WIN]) for i in range(len(waves))]


def transform(waves, right, left):
    return left_pass(right_pass(waves, right), left)


def transform_back(waves, right, left):
    return right_pass(left_pass(waves, left), right)


def crop(ref, layer, group, shift, column):
    rows = jnp.concatenate([ref[layer, group + j] for j in range(SPAN // 8)], axis=0)
    rows = pltpu.roll(rows, lax.rem(TILE - column, TILE), 1)[:, :WIN]
    return pltpu.roll(rows, lax.rem(SPAN - shift, SPAN), 0)[:WIN]


def add_all(values):
    total = values[0]
    for value in values[1:]:
        total = total + value
    return total


def spread_out(value, shift, column):
    tall = jnp.concatenate([value, jnp.zeros((SPAN - WIN, WIN), value.dtype)], axis=0)
    tall = pltpu.roll(tall, shift, 0)
    return pltpu.roll(jnp.concatenate([tall, jnp.zeros_like(tall)], axis=1), column, 1)


def sum_modes(pairs):
    return add_all([v[0] for v in pairs]), add_all([v[1] for v in pairs])


def fused_kernel(
    off_ref, count_ref, amp_ref, phase_ref, probe_ref, measured_ref, tables_ref, kernel_ref, out_ref,
    pad, grad, pair, half, xin, block, zin, total, strips, strips_in, rows_in, send, recv,
):
    tile, pos = lax.axis_index("tile"), lax.axis_index("pos")
    tiles = lax.axis_size("tile")
    core, z_hi, x = lax.rem(pos, 2), lax.rem(pos // 2, 2), pos // 4
    z_lo = lax.rem(tile, 4)
    xs = [lax.rem(x + step, 4) for step in range(4)]

    def at(tile_step, x_, z_, core_):
        return {"tile": lax.rem(tile + tiles + tile_step, tiles), "pos": x_ * 4 + z_ * 2 + core_}

    sibling = at(0, x, z_hi, 1 - core)
    along_x = {step: at(0, xs[step], z_hi, core) for step in (1, 2, 3)}
    across = at(0, x, 1 - z_hi, core)
    after = at(1, x, jnp.where(z_lo == 3, 1 - z_hi, z_hi), core)
    before = at(-1, x, jnp.where(z_lo == 0, 1 - z_hi, z_hi), core)
    below = at(4, x, z_hi, core)
    above = at(-4, x, z_hi, core)

    partners = (sibling, along_x[1], along_x[3], along_x[2], across, after, before, below, above)
    barrier = pltpu.get_barrier_semaphore()
    for partner in partners:
        pl.semaphore_signal(barrier, inc=1, device_id=partner, device_id_type=MESH)

    started = []

    def push(chunk, index, src, dst, device):
        copy = pltpu.make_async_remote_copy(
            src_ref=src, dst_ref=dst, send_sem=send.at[chunk, index], recv_sem=recv.at[chunk, index],
            device_id=device, device_id_type=MESH,
        )
        copy.start()
        started.append(copy)
        return copy

    def rows_of(x_, core_):
        return pl.ds(pl.multiple_of(lax.rem(x_, 2) * 32 + core_ * 16, 16), 16)

    def flat(value):
        return value.reshape(EDGE, TILE)

    forward, inverse = tables_ref[0], tables_ref[1]
    slots = range(SLOTS)
    groups, shifts, columns = [], [], []
    lives = [(count_ref[0, 0] - slot).astype(jnp.float32) for slot in slots]
    lives = [jnp.clip(jnp.full((1, WIN), live), 0.0, 1.0) for live in lives]
    for slot in slots:
        row = off_ref[slot, 0]
        group = lax.shift_right_logical(row - lax.shift_right_logical(row, 7), 3)
        groups.append(group)
        shifts.append(row - group * 8)
        columns.append(off_ref[slot, 1])

    def kernel():
        return kernel_ref[0], kernel_ref[1]

    def probe(m):
        return probe_ref[0, m], probe_ref[1, m]

    def deposit(slot, layer, grads):
        for part in range(2):
            value = grads[part] * lives[slot]
            placed = spread_out(value, shifts[slot], columns[slot])
            pad[slot, part, layer, LEAD : LEAD + SPAN // 8] = placed.reshape(SPAN // 8, 8, TILE)

    def collect(layer):
        for part in range(2):
            for r in range(TILE // 8):
                first, second = [pad[slot, part, layer, LEAD - groups[slot] + r] for slot in slots]
                grad[layer, part, r // 8, r % 8 * 8 : r % 8 * 8 + 8, :] = first + second

    empty = jnp.zeros((LEAD, 8, TILE), jnp.float32)
    for slot in slots:
        for part in range(2):
            for layer in range(LAYERS):
                pad[slot, part, layer, 0:LEAD] = empty
                pad[slot, part, layer, LEAD + SPAN // 8 :] = empty

    def each(stage, *lists):
        return [stage(*items) for items in zip(*lists)]

    modes = range(MODES)
    layers = []
    for slot in slots:
        layers.append(
            [
                polar(
                    crop(amp_ref, layer, groups[slot], shifts[slot], columns[slot]),
                    crop(phase_ref, layer, groups[slot], shifts[slot], columns[slot]),
                )
                for layer in range(LAYERS)
            ]
        )
    waves = [[times(probe(m), layers[slot][0]) for m in modes] for slot in slots]
    waves = each(lambda w: right_pass(w, forward), waves)
    waves = each(lambda w: left_pass(w, inverse), waves)
    waves = each(lambda w: [times(v, kernel()) for v in w], waves)
    waves = each(lambda w: right_pass(w, inverse), waves)
    returned = each(lambda w: left_pass(w, forward), waves)
    waves = each(lambda w, o: [times(v, o[1]) for v in w], returned, layers)
    waves = each(lambda w: right_pass(w, forward), waves)
    far = each(lambda w: left_pass(w, inverse), waves)

    def pull(slot, w):
        misfit = add_all([re * re + im * im for re, im in w]) - measured_ref[slot]
        twice = misfit + misfit
        return [(twice * re, twice * im) for re, im in w]

    waves = each(pull, slots, far)
    waves = each(lambda w: left_pass(w, forward), waves)
    waves = each(lambda w: right_pass(w, inverse), waves)
    for slot in slots:
        deposit(slot, 1, sum_modes([times_conj(g, r) for g, r in zip(waves[slot], returned[slot])]))
    collect(1)

    def swap_pair(chunk):
        copies = []
        for step in (2, 1, 3, 0):
            owner = xs[step]
            src = grad.at[chunk, owner // 2, :, rows_of(owner, 1 - core)]
            copies.append((step, push(chunk, step, src, pair.at[chunk, step], sibling)))
        return copies

    def spread_x(chunk, swaps):
        copies = []
        for step, swap in swaps:
            swap.wait_recv()
            owner = xs[step]
            half[chunk, step] = grad[chunk, owner // 2, :, rows_of(owner, core), :] + pair[chunk, step]
            if step:
                copies.append(push(chunk, 3 + step, half.at[chunk, step], xin.at[chunk, step - 1], along_x[step]))
        return copies

    def swap_z(chunk, copies):
        for copy in copies:
            copy.wait_recv()
        block[chunk] = half[chunk, 0] + (xin[chunk, 0] + xin[chunk, 2] + xin[chunk, 1])
        return push(chunk, 7, block.at[chunk], zin.at[chunk], across)

    low = lax.broadcasted_iota(jnp.int32, (32, WIN), 1) < EDGE

    def swap_strips(chunk, copy):
        copy.wait_recv()
        total[chunk] = block[chunk] + zin[chunk]
        copies = [
            push(chunk, 8, total.at[chunk, 3], rows_in.at[chunk, 0], below),
            push(chunk, 9, total.at[chunk, 0], rows_in.at[chunk, 1], above),
        ]
        value = flat(total[chunk])
        left, right = value[:, :WIN], value[:, WIN:]
        strips[chunk, 0] = jnp.where(low, pltpu.roll(right[:32], EDGE, 1), right[32:])
        strips[chunk, 1] = jnp.where(low, left[:32], pltpu.roll(left[32:], EDGE, 1))
        copies.append(push(chunk, 10, strips.at[chunk, 0], strips_in.at[chunk, 0], after))
        copies.append(push(chunk, 11, strips.at[chunk, 1], strips_in.at[chunk, 1], before))
        return copies

    own_rows = rows_of(x, core)
    offset = lax.rem(x, 2) * 4 + core * 2

    def share(chunk, index, step, device):
        owner = xs[step]
        view = out_ref.at[owner // 2, chunk, :, rows_of(owner, core)]
        return push(chunk, index, view, view, device)

    def object_block(layer):
        def read(ref):
            return jnp.concatenate(
                [ref[layer, pl.ds(p * 8 + offset, 2)].reshape(16, TILE) for p in range(4)], axis=0
            )

        both = polar(read(amp_ref), read(phase_ref))
        return jnp.where(x < 2, both[0], both[1])

    def update(chunk, copies, base):
        for copy in copies:
            copy.wait_recv()
        from_left = jnp.where(tile > 0, strips_in[chunk, 0], 0.0)
        from_right = jnp.where(tile < tiles - 1, strips_in[chunk, 1], 0.0)
        left = jnp.concatenate(
            [jnp.where(low, from_left, 0.0), jnp.where(low, pltpu.roll(from_left, EDGE, 1), 0.0)], axis=0
        )
        right = jnp.concatenate(
            [jnp.where(low, 0.0, pltpu.roll(from_right, EDGE, 1)), jnp.where(low, 0.0, from_right)], axis=0
        )
        top = jnp.where(tile >= 4, rows_in[chunk, 0], 0.0)
        bottom = jnp.where(tile < tiles - 4, rows_in[chunk, 1], 0.0)
        ends = jnp.concatenate([top, jnp.zeros((32, TILE), jnp.float32), bottom], axis=0)
        combined = flat(total[chunk]) + jnp.concatenate([left, right], axis=1) + ends
        out_ref[x // 2, chunk, :, own_rows, :] = (base - STEP * combined).reshape(4, 16, TILE)
        remote = [(step, share(chunk, 11 + step, 0, along_x[step])) for step in (2, 1, 3)]
        return remote, [share(chunk, 15, 0, sibling)]

    def relay(chunk, remote, local):
        for step, copy in remote:
            copy.wait_recv()
            local.append(share(chunk, 15 + step, 4 - step, sibling))

    pl.semaphore_wait(barrier, len(partners))
    pairs_late = swap_pair(1)
    waves = each(lambda w, o: [times_conj(v, o[1]) for v in w], waves, layers)
    waves = each(lambda w: left_pass(w, inverse), waves)
    waves = each(lambda w: right_pass(w, forward), waves)
    waves = each(lambda w: [times_conj(v, kernel()) for v in w], waves)
    xs_late = spread_x(1, pairs_late)
    waves = each(lambda w: left_pass(w, forward), waves)
    waves = each(lambda w: right_pass(w, inverse), waves)
    for slot in slots:
        deposit(slot, 0, sum_modes([times_conj(waves[slot][m], probe(m)) for m in modes]))
    collect(0)
    pairs_early = swap_pair(0)
    z_late = swap_z(1, xs_late)
    xs_early = spread_x(0, pairs_early)
    base_late = object_block(1)
    z_early = swap_z(0, xs_early)
    base_early = object_block(0)
    strips_late = swap_strips(1, z_late)
    strips_early = swap_strips(0, z_early)
    remote_late, local_late = update(1, strips_late, base_late)
    remote_early, local_early = update(0, strips_early, base_early)
    relay(1, remote_late, local_late)
    relay(0, remote_early, local_early)
    for copy in local_late + local_early:
        copy.wait_recv()
    for copy in started:
        copy.wait_send()


def grouped(tile_array):
    return tile_array.reshape(LAYERS, TILE // 8, 8, TILE)


def per_device(amplitude, phase_map, probe_modes, offsets, pos_counts, measured):
    tables, kernel = make_tables()
    vmem = pl.BlockSpec(memory_space=pltpu.VMEM)
    smem = pl.BlockSpec(memory_space=pltpu.SMEM)
    f32 = jnp.float32
    updated = pl.pallas_call(
        fused_kernel,
        out_shape=jax.ShapeDtypeStruct((2, LAYERS, 4, EDGE, TILE), f32),
        in_specs=[smem, smem] + [vmem] * 6,
        out_specs=vmem,
        scratch_shapes=[
            pltpu.VMEM((SLOTS, 2, LAYERS, 2 * LEAD + SPAN // 8, 8, TILE), f32),
            pltpu.VMEM((LAYERS, 2, 4, EDGE, TILE), f32),
            pltpu.VMEM((LAYERS, 4, 4, 16, TILE), f32),
            pltpu.VMEM((LAYERS, 4, 4, 16, TILE), f32),
            pltpu.VMEM((LAYERS, 3, 4, 16, TILE), f32),
            pltpu.VMEM((LAYERS, 4, 16, TILE), f32),
            pltpu.VMEM((LAYERS, 4, 16, TILE), f32),
            pltpu.VMEM((LAYERS, 4, 16, TILE), f32),
            pltpu.VMEM((LAYERS, 2, 32, WIN), f32),
            pltpu.VMEM((LAYERS, 2, 32, WIN), f32),
            pltpu.VMEM((LAYERS, 2, 16, TILE), f32),
            pltpu.SemaphoreType.DMA((LAYERS, 19)),
            pltpu.SemaphoreType.DMA((LAYERS, 19)),
        ],
        compiler_params=pltpu.CompilerParams(collective_id=0, has_side_effects=True),
        name="gradient_and_combine",
    )(offsets[0], pos_counts, grouped(amplitude), grouped(phase_map), probe_modes, measured[0], jnp.asarray(tables), jnp.asarray(kernel))
    return updated.reshape(1, 2, LAYERS, TILE, TILE)


def solution(mesh):
    in_specs = (
        P("tile", None, None, None),
        P("tile", None, None, None),
        P(),
        P("tile", "pos", None),
        P("tile", "pos"),
        P("tile", "pos", None, None),
    )
    out_specs = P("tile", None, None, None, None)
    return jax.shard_map(per_device, mesh=mesh, in_specs=in_specs, out_specs=out_specs, check_vma=False)
```

```python
import functools
import math

import jax
import jax.numpy as jnp
import numpy as np
from jax import lax
from jax.experimental import pallas as pl
from jax.experimental.pallas import tpu as pltpu
from jax.sharding import PartitionSpec as P

MESH = pl.DeviceIdType.MESH
TILE = 256
WIN = 128
EDGE = 64
MODES = 3
LAYERS = 2
SLOTS = 2
SPAN = WIN + 8
LEAD = (TILE - SPAN) // 8
SUBS = 2
HIGH = 16 // SUBS
CHUNKS = LAYERS * SUBS
STEP = 0.1
FRESNEL = 0.0123
SIN = (0.9999999957326958, -0.16666657991741893, 0.008333051059307331, -0.0001980907498047039, 2.605224199925007e-06)
COS = (0.9999999997806426, -0.49999999358456015, 0.04166663625748454, -0.001388836139270363, 2.476016095941152e-05, -2.6051488147238807e-07)


def make_tables():
    counter = np.arange(WIN)
    angles = (np.outer(counter, counter) % WIN).astype(np.float32) * np.float32(2.0 * math.pi / WIN)
    scaling = np.float32(1.0 / math.sqrt(WIN))
    f_re = (np.cos(angles) * scaling).astype(jnp.bfloat16)
    f_im = (-np.sin(angles) * scaling).astype(jnp.bfloat16)
    forward = np.block([[f_re, f_im], [-f_im, f_re]])
    inverse = np.block([[f_re, -f_im], [f_im, f_re]])
    centered = ((counter + WIN // 2) % WIN - WIN // 2).astype(np.float32)
    square = centered * centered
    phases = np.float32(-FRESNEL) * (square[:, None] + square[None, :])
    kernel = np.stack([np.cos(phases), np.sin(phases)]).astype(np.float32)
    return np.stack([forward, inverse]).astype(jnp.bfloat16), kernel


def horner(terms, u):
    total = jnp.full_like(u, terms[-1])
    for term in terms[-2::-1]:
        total = total * u + term
    return total


def polar(amplitude, phase):
    half = phase * 0.5
    u = half * half
    sine = half * horner(SIN, u)
    cosine = horner(COS, u)
    return amplitude - (2.0 * amplitude) * (sine * sine), (2.0 * amplitude) * (sine * cosine)


def times(a, b):
    return a[0] * b[0] - a[1] * b[1], a[0] * b[1] + a[1] * b[0]


def times_conj(a, b):
    return a[0] * b[0] + a[1] * b[1], a[1] * b[0] - a[0] * b[1]


def right_pass(waves, table):
    rows = [jnp.concatenate([re.astype(jnp.bfloat16), im.astype(jnp.bfloat16)], axis=1) for re, im in waves]
    result = jnp.dot(jnp.concatenate(rows, axis=0), table, preferred_element_type=jnp.float32)
    return [(result[i * WIN : (i + 1) * WIN, :WIN], result[i * WIN : (i + 1) * WIN, WIN:]) for i in range(len(waves))]


def left_pass(waves, table):
    columns = [jnp.concatenate([re.astype(jnp.bfloat16), im.astype(jnp.bfloat16)], axis=0) for re, im in waves]
    result = jnp.dot(table, jnp.concatenate(columns, axis=1), preferred_element_type=jnp.float32)
    return [(result[:WIN, i * WIN : (i + 1) * WIN], result[WIN:, i * WIN : (i + 1) * WIN]) for i in range(len(waves))]


def transform(waves, right, left):
    return left_pass(right_pass(waves, right), left)


def transform_back(waves, right, left):
    return right_pass(left_pass(waves, left), right)


def crop(ref, layer, group, shift, column):
    rows = jnp.concatenate([ref[layer, group + j] for j in range(SPAN // 8)], axis=0)
    rows = pltpu.roll(rows, lax.rem(TILE - column, TILE), 1)[:, :WIN]
    return pltpu.roll(rows, lax.rem(SPAN - shift, SPAN), 0)[:WIN]


def add_all(values):
    total = values[0]
    for value in values[1:]:
        total = total + value
    return total


def spread_out(value, shift, column):
    tall = jnp.concatenate([value, jnp.zeros((SPAN - WIN, WIN), value.dtype)], axis=0)
    tall = pltpu.roll(tall, shift, 0)
    return pltpu.roll(jnp.concatenate([tall, jnp.zeros_like(tall)], axis=1), column, 1)


def sum_modes(pairs):
    return add_all([v[0] for v in pairs]), add_all([v[1] for v in pairs])


def fused_kernel(
    off_ref, count_ref, amp_ref, phase_ref, probe_ref, measured_ref, tables_ref, kernel_ref, out_ref,
    pad, grad, pair, half, xin, block, zin, total, strips, strips_in, rows_in, send, recv,
):
    tile, pos = lax.axis_index("tile"), lax.axis_index("pos")
    tiles = lax.axis_size("tile")
    core, z_hi, x = lax.rem(pos, 2), lax.rem(pos // 2, 2), pos // 4
    z_lo = lax.rem(tile, 4)
    xs = [lax.rem(x + step, 4) for step in range(4)]

    def at(tile_step, x_, z_, core_):
        return {"tile": lax.rem(tile + tiles + tile_step, tiles), "pos": x_ * 4 + z_ * 2 + core_}

    sibling = at(0, x, z_hi, 1 - core)
    along_x = {step: at(0, xs[step], z_hi, core) for step in (1, 2, 3)}
    across = at(0, x, 1 - z_hi, core)
    after = at(1, x, jnp.where(z_lo == 3, 1 - z_hi, z_hi), core)
    before = at(-1, x, jnp.where(z_lo == 0, 1 - z_hi, z_hi), core)
    below = at(4, x, z_hi, core)
    above = at(-4, x, z_hi, core)

    partners = (sibling, along_x[1], along_x[3], along_x[2], across, after, before, below, above)
    barrier = pltpu.get_barrier_semaphore()
    for partner in partners:
        pl.semaphore_signal(barrier, inc=1, device_id=partner, device_id_type=MESH)

    started = []

    def push(chunk, index, src, dst, device):
        copy = pltpu.make_async_remote_copy(
            src_ref=src, dst_ref=dst, send_sem=send.at[chunk, index], recv_sem=recv.at[chunk, index],
            device_id=device, device_id_type=MESH,
        )
        copy.start()
        started.append(copy)
        return copy

    def rows_of(x_, core_, sub):
        return pl.ds(pl.multiple_of(lax.rem(x_, 2) * 32 + core_ * 16 + sub * HIGH, HIGH), HIGH)

    def flat(value):
        return value.reshape(4 * HIGH, TILE)

    forward, inverse = tables_ref[0], tables_ref[1]
    slots = range(SLOTS)
    groups, shifts, columns = [], [], []
    lives = [(count_ref[0, 0] - slot).astype(jnp.float32) for slot in slots]
    lives = [jnp.clip(jnp.full((1, WIN), live), 0.0, 1.0) for live in lives]
    for slot in slots:
        row = off_ref[slot, 0]
        group = lax.shift_right_logical(row - lax.shift_right_logical(row, 7), 3)
        groups.append(group)
        shifts.append(row - group * 8)
        columns.append(off_ref[slot, 1])

    def kernel():
        return kernel_ref[0], kernel_ref[1]

    def probe(m):
        return probe_ref[0, m], probe_ref[1, m]

    def deposit(slot, layer, grads):
        for part in range(2):
            value = grads[part] * lives[slot]
            placed = spread_out(value, shifts[slot], columns[slot])
            pad[slot, part, layer, LEAD : LEAD + SPAN // 8] = placed.reshape(SPAN // 8, 8, TILE)

    def collect(layer):
        for part in range(2):
            for r in range(TILE // 8):
                first, second = [pad[slot, part, layer, LEAD - groups[slot] + r] for slot in slots]
                grad[layer, part, r // 8, r % 8 * 8 : r % 8 * 8 + 8, :] = first + second

    empty = jnp.zeros((LEAD, 8, TILE), jnp.float32)
    for slot in slots:
        for part in range(2):
            for layer in range(LAYERS):
                pad[slot, part, layer, 0:LEAD] = empty
                pad[slot, part, layer, LEAD + SPAN // 8 :] = empty

    def each(stage, *lists):
        return [stage(*items) for items in zip(*lists)]

    modes = range(MODES)
    layers = []
    for slot in slots:
        layers.append(
            [
                polar(
                    crop(amp_ref, layer, groups[slot], shifts[slot], columns[slot]),
                    crop(phase_ref, layer, groups[slot], shifts[slot], columns[slot]),
                )
                for layer in range(LAYERS)
            ]
        )
    waves = [[times(probe(m), layers[slot][0]) for m in modes] for slot in slots]
    waves = each(lambda w: right_pass(w, forward), waves)
    waves = each(lambda w: left_pass(w, inverse), waves)
    waves = each(lambda w: [times(v, kernel()) for v in w], waves)
    waves = each(lambda w: right_pass(w, inverse), waves)
    returned = each(lambda w: left_pass(w, forward), waves)
    waves = each(lambda w, o: [times(v, o[1]) for v in w], returned, layers)
    waves = each(lambda w: right_pass(w, forward), waves)
    far = each(lambda w: left_pass(w, inverse), waves)

    def pull(slot, w):
        misfit = add_all([re * re + im * im for re, im in w]) - measured_ref[slot]
        twice = misfit + misfit
        return [(twice * re, twice * im) for re, im in w]

    waves = each(pull, slots, far)
    waves = each(lambda w: left_pass(w, forward), waves)
    waves = each(lambda w: right_pass(w, inverse), waves)
    for slot in slots:
        deposit(slot, 1, sum_modes([times_conj(g, r) for g, r in zip(waves[slot], returned[slot])]))
    collect(1)

    def swap_pair(chunk):
        layer, sub = divmod(chunk, SUBS)
        copies = []
        for step in (2, 1, 3, 0):
            owner = xs[step]
            src = grad.at[layer, owner // 2, :, rows_of(owner, 1 - core, sub)]
            copies.append((step, push(chunk, step, src, pair.at[chunk, step], sibling)))
        return copies

    def spread_x(chunk, swaps):
        layer, sub = divmod(chunk, SUBS)
        copies = []
        for step, swap in swaps:
            swap.wait_recv()
            owner = xs[step]
            half[chunk, step] = grad[layer, owner // 2, :, rows_of(owner, core, sub), :] + pair[chunk, step]
            if step:
                copies.append(push(chunk, 3 + step, half.at[chunk, step], xin.at[chunk, step - 1], along_x[step]))
        return copies

    def swap_z(chunk, copies):
        for copy in copies:
            copy.wait_recv()
        block[chunk] = half[chunk, 0] + (xin[chunk, 0] + xin[chunk, 2] + xin[chunk, 1])
        return push(chunk, 7, block.at[chunk], zin.at[chunk], across)

    low = lax.broadcasted_iota(jnp.int32, (2 * HIGH, WIN), 1) < EDGE

    def swap_strips(chunk, copy):
        copy.wait_recv()
        total[chunk] = block[chunk] + zin[chunk]
        copies = [
            push(chunk, 8, total.at[chunk, 3], rows_in.at[chunk, 0], below),
            push(chunk, 9, total.at[chunk, 0], rows_in.at[chunk, 1], above),
        ]
        value = flat(total[chunk])
        left, right = value[:, :WIN], value[:, WIN:]
        strips[chunk, 0] = jnp.where(low, pltpu.roll(right[: 2 * HIGH], EDGE, 1), right[2 * HIGH :])
        strips[chunk, 1] = jnp.where(low, left[: 2 * HIGH], pltpu.roll(left[2 * HIGH :], EDGE, 1))
        copies.append(push(chunk, 10, strips.at[chunk, 0], strips_in.at[chunk, 0], after))
        copies.append(push(chunk, 11, strips.at[chunk, 1], strips_in.at[chunk, 1], before))
        return copies

    def share(chunk, index, step, device):
        layer, sub = divmod(chunk, SUBS)
        owner = xs[step]
        view = out_ref.at[owner // 2, layer, :, rows_of(owner, core, sub)]
        return push(chunk, index, view, view, device)

    def object_block(chunk):
        layer, sub = divmod(chunk, SUBS)
        first = lax.rem(x, 2) * 4 + core * 2 + sub * (HIGH // 8)

        def read(ref):
            return jnp.concatenate(
                [ref[layer, pl.ds(p * 8 + first, HIGH // 8)].reshape(HIGH, TILE) for p in range(4)], axis=0
            )

        both = polar(read(amp_ref), read(phase_ref))
        return jnp.where(x < 2, both[0], both[1])

    def update(chunk, copies, base):
        layer, sub = divmod(chunk, SUBS)
        for copy in copies:
            copy.wait_recv()
        from_left = jnp.where(tile > 0, strips_in[chunk, 0], 0.0)
        from_right = jnp.where(tile < tiles - 1, strips_in[chunk, 1], 0.0)
        left = jnp.concatenate(
            [jnp.where(low, from_left, 0.0), jnp.where(low, pltpu.roll(from_left, EDGE, 1), 0.0)], axis=0
        )
        right = jnp.concatenate(
            [jnp.where(low, 0.0, pltpu.roll(from_right, EDGE, 1)), jnp.where(low, 0.0, from_right)], axis=0
        )
        top = jnp.where(tile >= 4, rows_in[chunk, 0], 0.0)
        bottom = jnp.where(tile < tiles - 4, rows_in[chunk, 1], 0.0)
        ends = jnp.concatenate([top, jnp.zeros((2 * HIGH, TILE), jnp.float32), bottom], axis=0)
        combined = flat(total[chunk]) + jnp.concatenate([left, right], axis=1) + ends
        out_ref[x // 2, layer, :, rows_of(x, core, sub), :] = (base - STEP * combined).reshape(4, HIGH, TILE)
        remote = [(step, share(chunk, 11 + step, 0, along_x[step])) for step in (2, 1, 3)]
        return remote, [share(chunk, 15, 0, sibling)]

    def relay(chunk, remote, local):
        for step, copy in remote:
            copy.wait_recv()
            local.append(share(chunk, 15 + step, 4 - step, sibling))
        return local

    late = list(range(SUBS, CHUNKS))
    early = list(range(SUBS))
    order = late + early
    pl.semaphore_wait(barrier, len(partners))
    swaps = {chunk: swap_pair(chunk) for chunk in late}
    waves = each(lambda w, o: [times_conj(v, o[1]) for v in w], waves, layers)
    waves = each(lambda w: left_pass(w, inverse), waves)
    waves = each(lambda w: right_pass(w, forward), waves)
    waves = each(lambda w: [times_conj(v, kernel()) for v in w], waves)
    waves = each(lambda w: left_pass(w, forward), waves)
    sums = {chunk: spread_x(chunk, swaps[chunk]) for chunk in late}
    waves = each(lambda w: right_pass(w, inverse), waves)
    for slot in slots:
        deposit(slot, 0, sum_modes([times_conj(waves[slot][m], probe(m)) for m in modes]))
    collect(0)
    swaps.update({chunk: swap_pair(chunk) for chunk in early})
    bases = {chunk: object_block(chunk) for chunk in order}
    for chunk in early:
        sums[chunk] = spread_x(chunk, swaps[chunk])
    blocks = {chunk: swap_z(chunk, sums[chunk]) for chunk in order}
    edges = {chunk: swap_strips(chunk, blocks[chunk]) for chunk in order}
    shares = {chunk: update(chunk, edges[chunk], bases[chunk]) for chunk in order}
    ends = [relay(chunk, *shares[chunk]) for chunk in order]
    for local in ends:
        for copy in local:
            copy.wait_recv()
    for copy in started:
        copy.wait_send()


def grouped(tile_array):
    return tile_array.reshape(LAYERS, TILE // 8, 8, TILE)


def per_device(amplitude, phase_map, probe_modes, offsets, pos_counts, measured):
    tables, kernel = make_tables()
    vmem = pl.BlockSpec(memory_space=pltpu.VMEM)
    smem = pl.BlockSpec(memory_space=pltpu.SMEM)
    f32 = jnp.float32
    updated = pl.pallas_call(
        fused_kernel,
        out_shape=pltpu.VMEM((2, LAYERS, 4, EDGE, TILE), f32),
        in_specs=[smem, smem] + [vmem] * 6,
        out_specs=vmem,
        scratch_shapes=[
            pltpu.VMEM((SLOTS, 2, LAYERS, 2 * LEAD + SPAN // 8, 8, TILE), f32),
            pltpu.VMEM((LAYERS, 2, 4, EDGE, TILE), f32),
            pltpu.VMEM((CHUNKS, 4, 4, HIGH, TILE), f32),
            pltpu.VMEM((CHUNKS, 4, 4, HIGH, TILE), f32),
            pltpu.VMEM((CHUNKS, 3, 4, HIGH, TILE), f32),
            pltpu.VMEM((CHUNKS, 4, HIGH, TILE), f32),
            pltpu.VMEM((CHUNKS, 4, HIGH, TILE), f32),
            pltpu.VMEM((CHUNKS, 4, HIGH, TILE), f32),
            pltpu.VMEM((CHUNKS, 2, 2 * HIGH, WIN), f32),
            pltpu.VMEM((CHUNKS, 2, 2 * HIGH, WIN), f32),
            pltpu.VMEM((CHUNKS, 2, HIGH, TILE), f32),
            pltpu.SemaphoreType.DMA((CHUNKS, 19)),
            pltpu.SemaphoreType.DMA((CHUNKS, 19)),
        ],
        compiler_params=pltpu.CompilerParams(collective_id=0, has_side_effects=True),
        name="gradient_and_combine",
    )(offsets[0], pos_counts, grouped(amplitude), grouped(phase_map), probe_modes, measured[0], jnp.asarray(tables), jnp.asarray(kernel))
    return updated.reshape(1, 2, LAYERS, TILE, TILE)


def solution(mesh):
    in_specs = (
        P("tile", None, None, None),
        P("tile", None, None, None),
        P(),
        P("tile", "pos", None),
        P("tile", "pos"),
        P("tile", "pos", None, None),
    )
    out_specs = P("tile", None, None, None, None)
    return jax.shard_map(per_device, mesh=mesh, in_specs=in_specs, out_specs=out_specs, check_vma=False)
```

```python
import functools
import math

import jax
import jax.numpy as jnp
import numpy as np
from jax import lax
from jax.experimental import pallas as pl
from jax.experimental.pallas import tpu as pltpu
from jax.sharding import PartitionSpec as P

MESH = pl.DeviceIdType.MESH
TILE = 256
WIN = 128
EDGE = 64
MODES = 3
LAYERS = 2
SLOTS = 2
SPAN = WIN + 8
LEAD = (TILE - SPAN) // 8
SUBS = 2
HIGH = 16 // SUBS
CHUNKS = LAYERS * SUBS
STEP = 0.1
FRESNEL = 0.0123
SIN = (0.9999999957326958, -0.16666657991741893, 0.008333051059307331, -0.0001980907498047039, 2.605224199925007e-06)
COS = (0.9999999997806426, -0.49999999358456015, 0.04166663625748454, -0.001388836139270363, 2.476016095941152e-05, -2.6051488147238807e-07)


def make_tables():
    counter = np.arange(WIN)
    angles = (np.outer(counter, counter) % WIN).astype(np.float32) * np.float32(2.0 * math.pi / WIN)
    scaling = np.float32(1.0 / math.sqrt(WIN))
    f_re = (np.cos(angles) * scaling).astype(jnp.bfloat16)
    f_im = (-np.sin(angles) * scaling).astype(jnp.bfloat16)
    forward = np.block([[f_re, f_im], [-f_im, f_re]])
    inverse = np.block([[f_re, -f_im], [f_im, f_re]])
    centered = ((counter + WIN // 2) % WIN - WIN // 2).astype(np.float32)
    square = centered * centered
    phases = np.float32(-FRESNEL) * (square[:, None] + square[None, :])
    kernel = np.stack([np.cos(phases), np.sin(phases)]).astype(np.float32)
    return np.stack([forward, inverse]).astype(jnp.bfloat16), kernel


def horner(terms, u):
    total = jnp.full_like(u, terms[-1])
    for term in terms[-2::-1]:
        total = total * u + term
    return total


def polar(amplitude, phase):
    half = phase * 0.5
    u = half * half
    sine = half * horner(SIN, u)
    cosine = horner(COS, u)
    return amplitude - (2.0 * amplitude) * (sine * sine), (2.0 * amplitude) * (sine * cosine)


def times(a, b):
    return a[0] * b[0] - a[1] * b[1], a[0] * b[1] + a[1] * b[0]


def times_conj(a, b):
    return a[0] * b[0] + a[1] * b[1], a[1] * b[0] - a[0] * b[1]


def right_pass(waves, table):
    rows = [jnp.concatenate([re.astype(jnp.bfloat16), im.astype(jnp.bfloat16)], axis=1) for re, im in waves]
    result = jnp.dot(jnp.concatenate(rows, axis=0), table, preferred_element_type=jnp.float32)
    return [(result[i * WIN : (i + 1) * WIN, :WIN], result[i * WIN : (i + 1) * WIN, WIN:]) for i in range(len(waves))]


def left_pass(waves, table):
    columns = [jnp.concatenate([re.astype(jnp.bfloat16), im.astype(jnp.bfloat16)], axis=0) for re, im in waves]
    result = jnp.dot(table, jnp.concatenate(columns, axis=1), preferred_element_type=jnp.float32)
    return [(result[:WIN, i * WIN : (i + 1) * WIN], result[WIN:, i * WIN : (i + 1) * WIN]) for i in range(len(waves))]


def transform(waves, right, left):
    return left_pass(right_pass(waves, right), left)


def transform_back(waves, right, left):
    return right_pass(left_pass(waves, left), right)


def crop(ref, layer, group, shift, column):
    lane = lax.broadcasted_iota(jnp.int32, (8, WIN), 1)
    sublane = lax.broadcasted_iota(jnp.int32, (8, WIN), 0)
    rows = []
    for j in range(SPAN // 8):
        row = ref[layer, group + j]
        rows.append(pltpu.roll(jnp.where(lane >= column, row[:, :WIN], row[:, WIN:]), (WIN - column) & (WIN - 1), 1))
    picked = [
        pltpu.roll(jnp.where(sublane >= shift, rows[j], rows[j + 1]), (8 - shift) & 7, 0) for j in range(WIN // 8)
    ]
    return jnp.concatenate(picked, axis=0)


def add_all(values):
    total = values[0]
    for value in values[1:]:
        total = total + value
    return total


def spread_out(value, shift, column):
    lane = lax.broadcasted_iota(jnp.int32, (8, WIN), 1)
    sublane = lax.broadcasted_iota(jnp.int32, (8, WIN), 0)
    zero = jnp.zeros((8, WIN), jnp.float32)
    turned = [pltpu.roll(value[8 * j : 8 * j + 8], shift & 7, 0) for j in range(WIN // 8)]
    placed = []
    for j in range(SPAN // 8):
        before = turned[j - 1] if j else zero
        after = turned[j] if j < WIN // 8 else zero
        row = pltpu.roll(jnp.where(sublane >= shift, after, before), column & (WIN - 1), 1)
        placed.append(jnp.concatenate([jnp.where(lane >= column, row, 0.0), jnp.where(lane >= column, 0.0, row)], axis=1))
    return placed


def sum_modes(pairs):
    return add_all([v[0] for v in pairs]), add_all([v[1] for v in pairs])


def fused_kernel(
    off_ref, count_ref, amp_ref, phase_ref, probe_ref, measured_ref, tables_ref, kernel_ref, out_ref,
    pad, grad, pair, half, xin, block, zin, total, strips, strips_in, rows_in, send, recv,
):
    tile, pos = lax.axis_index("tile"), lax.axis_index("pos")
    tiles = lax.axis_size("tile")
    core, z_hi, x = lax.rem(pos, 2), lax.rem(pos // 2, 2), pos // 4
    z_lo = lax.rem(tile, 4)
    xs = [lax.rem(x + step, 4) for step in range(4)]

    def at(tile_step, x_, z_, core_):
        return {"tile": lax.rem(tile + tiles + tile_step, tiles), "pos": x_ * 4 + z_ * 2 + core_}

    sibling = at(0, x, z_hi, 1 - core)
    along_x = {step: at(0, xs[step], z_hi, core) for step in (1, 2, 3)}
    across = at(0, x, 1 - z_hi, core)
    after = at(1, x, jnp.where(z_lo == 3, 1 - z_hi, z_hi), core)
    before = at(-1, x, jnp.where(z_lo == 0, 1 - z_hi, z_hi), core)
    below = at(4, x, z_hi, core)
    above = at(-4, x, z_hi, core)

    partners = (sibling, along_x[1], along_x[3], along_x[2], across, after, before, below, above)
    barrier = pltpu.get_barrier_semaphore()
    for partner in partners:
        pl.semaphore_signal(barrier, inc=1, device_id=partner, device_id_type=MESH)

    started = []

    def push(chunk, index, src, dst, device):
        copy = pltpu.make_async_remote_copy(
            src_ref=src, dst_ref=dst, send_sem=send.at[chunk, index], recv_sem=recv.at[chunk, index],
            device_id=device, device_id_type=MESH,
        )
        copy.start()
        started.append(copy)
        return copy

    def rows_of(x_, core_, sub):
        return pl.ds(pl.multiple_of(lax.rem(x_, 2) * 32 + core_ * 16 + sub * HIGH, HIGH), HIGH)

    def flat(value):
        return value.reshape(4 * HIGH, TILE)

    forward, inverse = tables_ref[0], tables_ref[1]
    slots = range(SLOTS)
    groups, shifts, columns = [], [], []
    lives = [(count_ref[0, 0] - slot).astype(jnp.float32) for slot in slots]
    lives = [jnp.clip(jnp.full((1, WIN), live), 0.0, 1.0) for live in lives]
    for slot in slots:
        row = off_ref[slot, 0]
        group = lax.shift_right_logical(row - lax.shift_right_logical(row, 7), 3)
        groups.append(group)
        shifts.append(row - group * 8)
        columns.append(off_ref[slot, 1])

    def kernel():
        return kernel_ref[0], kernel_ref[1]

    def probe(m):
        return probe_ref[0, m], probe_ref[1, m]

    def deposit(slot, layer, grads):
        for part in range(2):
            value = grads[part] * lives[slot]
            for j, row in enumerate(spread_out(value, shifts[slot], columns[slot])):
                pad[slot, part, layer, LEAD + j] = row

    def collect(layer):
        for part in range(2):
            for r in range(TILE // 8):
                first, second = [pad[slot, part, layer, LEAD - groups[slot] + r] for slot in slots]
                grad[layer, part, r // 8, r % 8 * 8 : r % 8 * 8 + 8, :] = first + second

    empty = jnp.zeros((LEAD, 8, TILE), jnp.float32)
    for slot in slots:
        for part in range(2):
            for layer in range(LAYERS):
                pad[slot, part, layer, 0:LEAD] = empty
                pad[slot, part, layer, LEAD + SPAN // 8 :] = empty

    def each(stage, *lists):
        return [stage(*items) for items in zip(*lists)]

    modes = range(MODES)
    layers = []
    for slot in slots:
        layers.append(
            [
                polar(
                    crop(amp_ref, layer, groups[slot], shifts[slot], columns[slot]),
                    crop(phase_ref, layer, groups[slot], shifts[slot], columns[slot]),
                )
                for layer in range(LAYERS)
            ]
        )
    waves = [[times(probe(m), layers[slot][0]) for m in modes] for slot in slots]
    waves = each(lambda w: right_pass(w, forward), waves)
    waves = each(lambda w: left_pass(w, inverse), waves)
    waves = each(lambda w: [times(v, kernel()) for v in w], waves)
    waves = each(lambda w: right_pass(w, inverse), waves)
    returned = each(lambda w: left_pass(w, forward), waves)
    waves = each(lambda w, o: [times(v, o[1]) for v in w], returned, layers)
    waves = each(lambda w: right_pass(w, forward), waves)
    far = each(lambda w: left_pass(w, inverse), waves)

    def pull(slot, w):
        misfit = add_all([re * re + im * im for re, im in w]) - measured_ref[slot]
        twice = misfit + misfit
        return [(twice * re, twice * im) for re, im in w]

    waves = each(pull, slots, far)
    waves = each(lambda w: left_pass(w, forward), waves)
    waves = each(lambda w: right_pass(w, inverse), waves)
    for slot in slots:
        deposit(slot, 1, sum_modes([times_conj(g, r) for g, r in zip(waves[slot], returned[slot])]))
    collect(1)

    def swap_pair(chunk):
        layer, sub = divmod(chunk, SUBS)
        copies = []
        for step in (2, 1, 3, 0):
            owner = xs[step]
            src = grad.at[layer, owner // 2, :, rows_of(owner, 1 - core, sub)]
            copies.append((step, push(chunk, step, src, pair.at[chunk, step], sibling)))
        return copies

    def spread_x(chunk, swaps):
        layer, sub = divmod(chunk, SUBS)
        copies = []
        for step, swap in swaps:
            swap.wait_recv()
            owner = xs[step]
            half[chunk, step] = grad[layer, owner // 2, :, rows_of(owner, core, sub), :] + pair[chunk, step]
            if step:
                copies.append(push(chunk, 3 + step, half.at[chunk, step], xin.at[chunk, step - 1], along_x[step]))
        return copies

    def swap_z(chunk, copies):
        for copy in copies:
            copy.wait_recv()
        block[chunk] = half[chunk, 0] + (xin[chunk, 0] + xin[chunk, 2] + xin[chunk, 1])
        return push(chunk, 7, block.at[chunk], zin.at[chunk], across)

    low = lax.broadcasted_iota(jnp.int32, (2 * HIGH, WIN), 1) < EDGE

    def swap_strips(chunk, copy):
        copy.wait_recv()
        total[chunk] = block[chunk] + zin[chunk]
        copies = [
            push(chunk, 8, total.at[chunk, 3], rows_in.at[chunk, 0], below),
            push(chunk, 9, total.at[chunk, 0], rows_in.at[chunk, 1], above),
        ]
        value = flat(total[chunk])
        left, right = value[:, :WIN], value[:, WIN:]
        strips[chunk, 0] = jnp.where(low, pltpu.roll(right[: 2 * HIGH], EDGE, 1), right[2 * HIGH :])
        strips[chunk, 1] = jnp.where(low, left[: 2 * HIGH], pltpu.roll(left[2 * HIGH :], EDGE, 1))
        copies.append(push(chunk, 10, strips.at[chunk, 0], strips_in.at[chunk, 0], after))
        copies.append(push(chunk, 11, strips.at[chunk, 1], strips_in.at[chunk, 1], before))
        return copies

    def share(chunk, index, step, device):
        layer, sub = divmod(chunk, SUBS)
        owner = xs[step]
        view = out_ref.at[owner // 2, layer, :, rows_of(owner, core, sub)]
        return push(chunk, index, view, view, device)

    def object_block(chunk):
        layer, sub = divmod(chunk, SUBS)
        first = lax.rem(x, 2) * 4 + core * 2 + sub * (HIGH // 8)

        def read(ref):
            return jnp.concatenate(
                [ref[layer, pl.ds(p * 8 + first, HIGH // 8)].reshape(HIGH, TILE) for p in range(4)], axis=0
            )

        both = polar(read(amp_ref), read(phase_ref))
        return jnp.where(x < 2, both[0], both[1])

    def update(chunk, copies, base):
        layer, sub = divmod(chunk, SUBS)
        for copy in copies:
            copy.wait_recv()
        from_left = jnp.where(tile > 0, strips_in[chunk, 0], 0.0)
        from_right = jnp.where(tile < tiles - 1, strips_in[chunk, 1], 0.0)
        left = jnp.concatenate(
            [jnp.where(low, from_left, 0.0), jnp.where(low, pltpu.roll(from_left, EDGE, 1), 0.0)], axis=0
        )
        right = jnp.concatenate(
            [jnp.where(low, 0.0, pltpu.roll(from_right, EDGE, 1)), jnp.where(low, 0.0, from_right)], axis=0
        )
        top = jnp.where(tile >= 4, rows_in[chunk, 0], 0.0)
        bottom = jnp.where(tile < tiles - 4, rows_in[chunk, 1], 0.0)
        ends = jnp.concatenate([top, jnp.zeros((2 * HIGH, TILE), jnp.float32), bottom], axis=0)
        combined = flat(total[chunk]) + jnp.concatenate([left, right], axis=1) + ends
        out_ref[x // 2, layer, :, rows_of(x, core, sub), :] = (base - STEP * combined).reshape(4, HIGH, TILE)
        remote = [(step, share(chunk, 11 + step, 0, along_x[step])) for step in (2, 1, 3)]
        return remote, [share(chunk, 15, 0, sibling)]

    def relay(chunk, remote, local):
        for step, copy in remote:
            copy.wait_recv()
            local.append(share(chunk, 15 + step, 4 - step, sibling))
        return local

    late = list(range(SUBS, CHUNKS))
    early = list(range(SUBS))
    order = late + early
    pl.semaphore_wait(barrier, len(partners))
    swaps = {chunk: swap_pair(chunk) for chunk in late}
    waves = each(lambda w, o: [times_conj(v, o[1]) for v in w], waves, layers)
    waves = each(lambda w: left_pass(w, inverse), waves)
    waves = each(lambda w: right_pass(w, forward), waves)
    waves = each(lambda w: [times_conj(v, kernel()) for v in w], waves)
    waves = each(lambda w: left_pass(w, forward), waves)
    waves = each(lambda w: right_pass(w, inverse), waves)
    sums = {chunk: spread_x(chunk, swaps[chunk]) for chunk in late}
    for slot in slots:
        deposit(slot, 0, sum_modes([times_conj(waves[slot][m], probe(m)) for m in modes]))
    collect(0)
    swaps.update({chunk: swap_pair(chunk) for chunk in early})
    bases = {chunk: object_block(chunk) for chunk in order}
    for chunk in early:
        sums[chunk] = spread_x(chunk, swaps[chunk])
    blocks = {chunk: swap_z(chunk, sums[chunk]) for chunk in order}
    edges = {chunk: swap_strips(chunk, blocks[chunk]) for chunk in order}
    shares = {chunk: update(chunk, edges[chunk], bases[chunk]) for chunk in order}
    ends = [relay(chunk, *shares[chunk]) for chunk in order]
    for local in ends:
        for copy in local:
            copy.wait_recv()
    for copy in started:
        copy.wait_send()


def grouped(tile_array):
    return tile_array.reshape(LAYERS, TILE // 8, 8, TILE)


def per_device(amplitude, phase_map, probe_modes, offsets, pos_counts, measured):
    tables, kernel = make_tables()
    vmem = pl.BlockSpec(memory_space=pltpu.VMEM)
    smem = pl.BlockSpec(memory_space=pltpu.SMEM)
    f32 = jnp.float32
    updated = pl.pallas_call(
        fused_kernel,
        out_shape=pltpu.VMEM((2, LAYERS, 4, EDGE, TILE), f32),
        in_specs=[smem, smem] + [vmem] * 6,
        out_specs=vmem,
        scratch_shapes=[
            pltpu.VMEM((SLOTS, 2, LAYERS, 2 * LEAD + SPAN // 8, 8, TILE), f32),
            pltpu.VMEM((LAYERS, 2, 4, EDGE, TILE), f32),
            pltpu.VMEM((CHUNKS, 4, 4, HIGH, TILE), f32),
            pltpu.VMEM((CHUNKS, 4, 4, HIGH, TILE), f32),
            pltpu.VMEM((CHUNKS, 3, 4, HIGH, TILE), f32),
            pltpu.VMEM((CHUNKS, 4, HIGH, TILE), f32),
            pltpu.VMEM((CHUNKS, 4, HIGH, TILE), f32),
            pltpu.VMEM((CHUNKS, 4, HIGH, TILE), f32),
            pltpu.VMEM((CHUNKS, 2, 2 * HIGH, WIN), f32),
            pltpu.VMEM((CHUNKS, 2, 2 * HIGH, WIN), f32),
            pltpu.VMEM((CHUNKS, 2, HIGH, TILE), f32),
            pltpu.SemaphoreType.DMA((CHUNKS, 19)),
            pltpu.SemaphoreType.DMA((CHUNKS, 19)),
        ],
        compiler_params=pltpu.CompilerParams(collective_id=0, has_side_effects=True),
        name="gradient_and_combine",
    )(offsets[0], pos_counts, grouped(amplitude), grouped(phase_map), probe_modes, measured[0], jnp.asarray(tables), jnp.asarray(kernel))
    return updated.reshape(1, 2, LAYERS, TILE, TILE)


def solution(mesh):
    in_specs = (
        P("tile", None, None, None),
        P("tile", None, None, None),
        P(),
        P("tile", "pos", None),
        P("tile", "pos"),
        P("tile", "pos", None, None),
    )
    out_specs = P("tile", None, None, None, None)
    return jax.shard_map(per_device, mesh=mesh, in_specs=in_specs, out_specs=out_specs, check_vma=False)
```

```python
import functools
import math

import jax
import jax.numpy as jnp
import numpy as np
from jax import lax
from jax.experimental import pallas as pl
from jax.experimental.pallas import tpu as pltpu
from jax.sharding import PartitionSpec as P

MESH = pl.DeviceIdType.MESH
TILE = 256
WIN = 128
EDGE = 64
MODES = 3
LAYERS = 2
SLOTS = 2
SPAN = WIN + 8
LEAD = (TILE - SPAN) // 8
SUBS = 2
HIGH = 16 // SUBS
CHUNKS = LAYERS * SUBS
STEP = 0.1
FRESNEL = 0.0123
SIN = (0.9999999957326958, -0.16666657991741893, 0.008333051059307331, -0.0001980907498047039, 2.605224199925007e-06)
COS = (0.9999999997806426, -0.49999999358456015, 0.04166663625748454, -0.001388836139270363, 2.476016095941152e-05, -2.6051488147238807e-07)


def make_tables():
    counter = np.arange(WIN)
    angles = (np.outer(counter, counter) % WIN).astype(np.float32) * np.float32(2.0 * math.pi / WIN)
    scaling = np.float32(1.0 / math.sqrt(WIN))
    f_re = (np.cos(angles) * scaling).astype(jnp.bfloat16)
    f_im = (-np.sin(angles) * scaling).astype(jnp.bfloat16)
    forward = np.block([[f_re, f_im], [-f_im, f_re]])
    inverse = np.block([[f_re, -f_im], [f_im, f_re]])
    centered = ((counter + WIN // 2) % WIN - WIN // 2).astype(np.float32)
    square = centered * centered
    phases = np.float32(-FRESNEL) * (square[:, None] + square[None, :])
    kernel = np.stack([np.cos(phases), np.sin(phases)]).astype(np.float32)
    return np.stack([forward, inverse]).astype(jnp.bfloat16), kernel


def horner(terms, u):
    total = jnp.full_like(u, terms[-1])
    for term in terms[-2::-1]:
        total = total * u + term
    return total


def polar(amplitude, phase):
    half = phase * 0.5
    u = half * half
    sine = half * horner(SIN, u)
    cosine = horner(COS, u)
    return amplitude - (2.0 * amplitude) * (sine * sine), (2.0 * amplitude) * (sine * cosine)


def times(a, b):
    return a[0] * b[0] - a[1] * b[1], a[0] * b[1] + a[1] * b[0]


def times_conj(a, b):
    return a[0] * b[0] + a[1] * b[1], a[1] * b[0] - a[0] * b[1]


def right_pass(waves, table):
    rows = [jnp.concatenate([re.astype(jnp.bfloat16), im.astype(jnp.bfloat16)], axis=1) for re, im in waves]
    result = jnp.dot(jnp.concatenate(rows, axis=0), table, preferred_element_type=jnp.float32)
    return [(result[i * WIN : (i + 1) * WIN, :WIN], result[i * WIN : (i + 1) * WIN, WIN:]) for i in range(len(waves))]


def left_pass(waves, table):
    columns = [jnp.concatenate([re.astype(jnp.bfloat16), im.astype(jnp.bfloat16)], axis=0) for re, im in waves]
    result = jnp.dot(table, jnp.concatenate(columns, axis=1), preferred_element_type=jnp.float32)
    return [(result[:WIN, i * WIN : (i + 1) * WIN], result[WIN:, i * WIN : (i + 1) * WIN]) for i in range(len(waves))]


def transform(waves, right, left):
    return left_pass(right_pass(waves, right), left)


def transform_back(waves, right, left):
    return right_pass(left_pass(waves, left), right)


def crop(ref, layer, group, shift, column):
    lane = lax.broadcasted_iota(jnp.int32, (8, WIN), 1)
    sublane = lax.broadcasted_iota(jnp.int32, (8, WIN), 0)
    rows = []
    for j in range(SPAN // 8):
        row = ref[layer, group + j]
        rows.append(pltpu.roll(jnp.where(lane >= column, row[:, :WIN], row[:, WIN:]), (WIN - column) & (WIN - 1), 1))
    picked = [
        pltpu.roll(jnp.where(sublane >= shift, rows[j], rows[j + 1]), (8 - shift) & 7, 0) for j in range(WIN // 8)
    ]
    return jnp.concatenate(picked, axis=0)


def add_all(values):
    total = values[0]
    for value in values[1:]:
        total = total + value
    return total


def spread_out(value, shift, column):
    lane = lax.broadcasted_iota(jnp.int32, (8, WIN), 1)
    sublane = lax.broadcasted_iota(jnp.int32, (8, WIN), 0)
    zero = jnp.zeros((8, WIN), jnp.float32)
    turned = [pltpu.roll(value[8 * j : 8 * j + 8], shift & 7, 0) for j in range(WIN // 8)]
    placed = []
    for j in range(SPAN // 8):
        before = turned[j - 1] if j else zero
        after = turned[j] if j < WIN // 8 else zero
        row = pltpu.roll(jnp.where(sublane >= shift, after, before), column & (WIN - 1), 1)
        placed.append(jnp.concatenate([jnp.where(lane >= column, row, 0.0), jnp.where(lane >= column, 0.0, row)], axis=1))
    return placed


def sum_modes(pairs):
    return add_all([v[0] for v in pairs]), add_all([v[1] for v in pairs])


def fused_kernel(
    off_ref, count_ref, amp_hbm, phase_hbm, probe_hbm, measured_hbm, tables_hbm, kernel_hbm, out_ref,
    amp_ref, phase_ref, probe_ref, measured_ref, tables_ref, kernel_ref, load_sem, pad, grad, pair, half, xin, block, zin, total, strips, strips_in, rows_in, send, recv,
):
    places = (
        (amp_hbm, amp_ref), (phase_hbm, phase_ref), (probe_hbm, probe_ref), (tables_hbm, tables_ref),
        (kernel_hbm, kernel_ref), (measured_hbm, measured_ref),
    )
    loads = [pltpu.make_async_copy(src, dst, load_sem.at[i]) for i, (src, dst) in enumerate(places)]
    for load in loads:
        load.start()
    tile, pos = lax.axis_index("tile"), lax.axis_index("pos")
    tiles = lax.axis_size("tile")
    core, z_hi, x = lax.rem(pos, 2), lax.rem(pos // 2, 2), pos // 4
    z_lo = lax.rem(tile, 4)
    xs = [lax.rem(x + step, 4) for step in range(4)]

    def at(tile_step, x_, z_, core_):
        return {"tile": lax.rem(tile + tiles + tile_step, tiles), "pos": x_ * 4 + z_ * 2 + core_}

    sibling = at(0, x, z_hi, 1 - core)
    along_x = {step: at(0, xs[step], z_hi, core) for step in (1, 2, 3)}
    across = at(0, x, 1 - z_hi, core)
    after = at(1, x, jnp.where(z_lo == 3, 1 - z_hi, z_hi), core)
    before = at(-1, x, jnp.where(z_lo == 0, 1 - z_hi, z_hi), core)
    below = at(4, x, z_hi, core)
    above = at(-4, x, z_hi, core)

    partners = (sibling, along_x[1], along_x[3], along_x[2], across, after, before, below, above)
    barrier = pltpu.get_barrier_semaphore()
    for partner in partners:
        pl.semaphore_signal(barrier, inc=1, device_id=partner, device_id_type=MESH)

    started = []

    def push(chunk, index, src, dst, device):
        copy = pltpu.make_async_remote_copy(
            src_ref=src, dst_ref=dst, send_sem=send.at[chunk, index], recv_sem=recv.at[chunk, index],
            device_id=device, device_id_type=MESH,
        )
        copy.start()
        started.append(copy)
        return copy

    def rows_of(x_, core_, sub):
        return pl.ds(pl.multiple_of(lax.rem(x_, 2) * 32 + core_ * 16 + sub * HIGH, HIGH), HIGH)

    def flat(value):
        return value.reshape(4 * HIGH, TILE)

    slots = range(SLOTS)
    groups, shifts, columns = [], [], []
    lives = [(count_ref[0, 0] - slot).astype(jnp.float32) for slot in slots]
    lives = [jnp.clip(jnp.full((1, WIN), live), 0.0, 1.0) for live in lives]
    for slot in slots:
        row = off_ref[slot, 0]
        group = lax.shift_right_logical(row - lax.shift_right_logical(row, 7), 3)
        groups.append(group)
        shifts.append(row - group * 8)
        columns.append(off_ref[slot, 1])

    def kernel():
        return kernel_ref[0], kernel_ref[1]

    def probe(m):
        return probe_ref[0, m], probe_ref[1, m]

    def deposit(slot, layer, grads):
        for part in range(2):
            value = grads[part] * lives[slot]
            for j, row in enumerate(spread_out(value, shifts[slot], columns[slot])):
                pad[slot, part, layer, LEAD + j] = row

    def collect(layer):
        for part in range(2):
            for r in range(TILE // 8):
                first, second = [pad[slot, part, layer, LEAD - groups[slot] + r] for slot in slots]
                grad[layer, part, r // 8, r % 8 * 8 : r % 8 * 8 + 8, :] = first + second

    empty = jnp.zeros((LEAD, 8, TILE), jnp.float32)
    for slot in slots:
        for part in range(2):
            for layer in range(LAYERS):
                pad[slot, part, layer, 0:LEAD] = empty
                pad[slot, part, layer, LEAD + SPAN // 8 :] = empty

    def each(stage, *lists):
        return [stage(*items) for items in zip(*lists)]

    modes = range(MODES)
    def crop_layer(layer):
        return [
            polar(
                crop(amp_ref, layer, groups[slot], shifts[slot], columns[slot]),
                crop(phase_ref, layer, groups[slot], shifts[slot], columns[slot]),
            )
            for slot in slots
        ]

    loads[0].wait()
    loads[1].wait()
    layers = [crop_layer(0)]
    loads[2].wait()
    loads[3].wait()
    forward, inverse = tables_ref[0], tables_ref[1]
    waves = [[times(probe(m), layers[0][slot]) for m in modes] for slot in slots]
    for load in loads[4:]:
        load.wait()
    layers.append(crop_layer(1))
    layers = list(zip(*layers))
    waves = each(lambda w: right_pass(w, forward), waves)
    waves = each(lambda w: left_pass(w, inverse), waves)
    waves = each(lambda w: [times(v, kernel()) for v in w], waves)
    waves = each(lambda w: right_pass(w, inverse), waves)
    returned = each(lambda w: left_pass(w, forward), waves)
    waves = each(lambda w, o: [times(v, o[1]) for v in w], returned, layers)
    waves = each(lambda w: right_pass(w, forward), waves)
    far = each(lambda w: left_pass(w, inverse), waves)

    def pull(slot, w):
        misfit = add_all([re * re + im * im for re, im in w]) - measured_ref[slot]
        twice = misfit + misfit
        return [(twice * re, twice * im) for re, im in w]

    waves = each(pull, slots, far)
    waves = each(lambda w: left_pass(w, forward), waves)
    waves = each(lambda w: right_pass(w, inverse), waves)
    for slot in slots:
        deposit(slot, 1, sum_modes([times_conj(g, r) for g, r in zip(waves[slot], returned[slot])]))
    collect(1)

    def swap_pair(chunk):
        layer, sub = divmod(chunk, SUBS)
        copies = []
        for step in (2, 1, 3, 0):
            owner = xs[step]
            src = grad.at[layer, owner // 2, :, rows_of(owner, 1 - core, sub)]
            copies.append((step, push(chunk, step, src, pair.at[chunk, step], sibling)))
        return copies

    def spread_x(chunk, swaps):
        layer, sub = divmod(chunk, SUBS)
        copies = []
        for step, swap in swaps:
            swap.wait_recv()
            owner = xs[step]
            half[chunk, step] = grad[layer, owner // 2, :, rows_of(owner, core, sub), :] + pair[chunk, step]
            if step:
                copies.append(push(chunk, 3 + step, half.at[chunk, step], xin.at[chunk, step - 1], along_x[step]))
        return copies

    def swap_z(chunk, copies):
        for copy in copies:
            copy.wait_recv()
        block[chunk] = half[chunk, 0] + (xin[chunk, 0] + xin[chunk, 2] + xin[chunk, 1])
        return push(chunk, 7, block.at[chunk], zin.at[chunk], across)

    low = lax.broadcasted_iota(jnp.int32, (2 * HIGH, WIN), 1) < EDGE

    def swap_strips(chunk, copy):
        copy.wait_recv()
        total[chunk] = block[chunk] + zin[chunk]
        copies = [
            push(chunk, 8, total.at[chunk, 3], rows_in.at[chunk, 0], below),
            push(chunk, 9, total.at[chunk, 0], rows_in.at[chunk, 1], above),
        ]
        value = flat(total[chunk])
        left, right = value[:, :WIN], value[:, WIN:]
        strips[chunk, 0] = jnp.where(low, pltpu.roll(right[: 2 * HIGH], EDGE, 1), right[2 * HIGH :])
        strips[chunk, 1] = jnp.where(low, left[: 2 * HIGH], pltpu.roll(left[2 * HIGH :], EDGE, 1))
        copies.append(push(chunk, 10, strips.at[chunk, 0], strips_in.at[chunk, 0], after))
        copies.append(push(chunk, 11, strips.at[chunk, 1], strips_in.at[chunk, 1], before))
        return copies

    def share(chunk, index, step, device):
        layer, sub = divmod(chunk, SUBS)
        owner = xs[step]
        view = out_ref.at[owner // 2, layer, :, rows_of(owner, core, sub)]
        return push(chunk, index, view, view, device)

    def object_block(chunk):
        layer, sub = divmod(chunk, SUBS)
        first = lax.rem(x, 2) * 4 + core * 2 + sub * (HIGH // 8)

        def read(ref):
            return jnp.concatenate(
                [ref[layer, pl.ds(p * 8 + first, HIGH // 8)].reshape(HIGH, TILE) for p in range(4)], axis=0
            )

        both = polar(read(amp_ref), read(phase_ref))
        return jnp.where(x < 2, both[0], both[1])

    def update(chunk, copies, base):
        layer, sub = divmod(chunk, SUBS)
        for copy in copies:
            copy.wait_recv()
        from_left = jnp.where(tile > 0, strips_in[chunk, 0], 0.0)
        from_right = jnp.where(tile < tiles - 1, strips_in[chunk, 1], 0.0)
        left = jnp.concatenate(
            [jnp.where(low, from_left, 0.0), jnp.where(low, pltpu.roll(from_left, EDGE, 1), 0.0)], axis=0
        )
        right = jnp.concatenate(
            [jnp.where(low, 0.0, pltpu.roll(from_right, EDGE, 1)), jnp.where(low, 0.0, from_right)], axis=0
        )
        top = jnp.where(tile >= 4, rows_in[chunk, 0], 0.0)
        bottom = jnp.where(tile < tiles - 4, rows_in[chunk, 1], 0.0)
        ends = jnp.concatenate([top, jnp.zeros((2 * HIGH, TILE), jnp.float32), bottom], axis=0)
        combined = flat(total[chunk]) + jnp.concatenate([left, right], axis=1) + ends
        out_ref[x // 2, layer, :, rows_of(x, core, sub), :] = (base - STEP * combined).reshape(4, HIGH, TILE)
        remote = [(step, share(chunk, 11 + step, 0, along_x[step])) for step in (2, 1, 3)]
        return remote, [share(chunk, 15, 0, sibling)]

    def relay(chunk, remote, local):
        for step, copy in remote:
            copy.wait_recv()
            local.append(share(chunk, 15 + step, 4 - step, sibling))
        return local

    late = list(range(SUBS, CHUNKS))
    early = list(range(SUBS))
    order = late + early
    pl.semaphore_wait(barrier, len(partners))
    swaps = {chunk: swap_pair(chunk) for chunk in late}
    waves = each(lambda w, o: [times_conj(v, o[1]) for v in w], waves, layers)
    waves = each(lambda w: left_pass(w, inverse), waves)
    waves = each(lambda w: right_pass(w, forward), waves)
    waves = each(lambda w: [times_conj(v, kernel()) for v in w], waves)
    waves = each(lambda w: left_pass(w, forward), waves)
    waves = each(lambda w: right_pass(w, inverse), waves)
    sums = {chunk: spread_x(chunk, swaps[chunk]) for chunk in late}
    for slot in slots:
        deposit(slot, 0, sum_modes([times_conj(waves[slot][m], probe(m)) for m in modes]))
    collect(0)
    swaps.update({chunk: swap_pair(chunk) for chunk in early})
    bases = {chunk: object_block(chunk) for chunk in order}
    for chunk in early:
        sums[chunk] = spread_x(chunk, swaps[chunk])
    blocks = {chunk: swap_z(chunk, sums[chunk]) for chunk in order}
    edges = {chunk: swap_strips(chunk, blocks[chunk]) for chunk in order}
    shares = {chunk: update(chunk, edges[chunk], bases[chunk]) for chunk in order}
    ends = [relay(chunk, *shares[chunk]) for chunk in order]
    for local in ends:
        for copy in local:
            copy.wait_recv()
    for copy in started:
        copy.wait_send()


def grouped(tile_array):
    return tile_array.reshape(LAYERS, TILE // 8, 8, TILE)


def per_device(amplitude, phase_map, probe_modes, offsets, pos_counts, measured):
    tables, kernel = make_tables()
    vmem = pl.BlockSpec(memory_space=pltpu.VMEM)
    smem = pl.BlockSpec(memory_space=pltpu.SMEM)
    f32 = jnp.float32
    updated = pl.pallas_call(
        fused_kernel,
        out_shape=pltpu.VMEM((2, LAYERS, 4, EDGE, TILE), f32),
        in_specs=[smem, smem] + [pl.BlockSpec(memory_space=pl.ANY)] * 6,
        out_specs=vmem,
        scratch_shapes=[
            pltpu.VMEM((LAYERS, TILE // 8, 8, TILE), f32),
            pltpu.VMEM((LAYERS, TILE // 8, 8, TILE), f32),
            pltpu.VMEM((2, MODES, WIN, WIN), f32),
            pltpu.VMEM((SLOTS, WIN, WIN), f32),
            pltpu.VMEM((2, TILE, TILE), jnp.bfloat16),
            pltpu.VMEM((2, WIN, WIN), f32),
            pltpu.SemaphoreType.DMA((6,)),
            pltpu.VMEM((SLOTS, 2, LAYERS, 2 * LEAD + SPAN // 8, 8, TILE), f32),
            pltpu.VMEM((LAYERS, 2, 4, EDGE, TILE), f32),
            pltpu.VMEM((CHUNKS, 4, 4, HIGH, TILE), f32),
            pltpu.VMEM((CHUNKS, 4, 4, HIGH, TILE), f32),
            pltpu.VMEM((CHUNKS, 3, 4, HIGH, TILE), f32),
            pltpu.VMEM((CHUNKS, 4, HIGH, TILE), f32),
            pltpu.VMEM((CHUNKS, 4, HIGH, TILE), f32),
            pltpu.VMEM((CHUNKS, 4, HIGH, TILE), f32),
            pltpu.VMEM((CHUNKS, 2, 2 * HIGH, WIN), f32),
            pltpu.VMEM((CHUNKS, 2, 2 * HIGH, WIN), f32),
            pltpu.VMEM((CHUNKS, 2, HIGH, TILE), f32),
            pltpu.SemaphoreType.DMA((CHUNKS, 19)),
            pltpu.SemaphoreType.DMA((CHUNKS, 19)),
        ],
        compiler_params=pltpu.CompilerParams(collective_id=0, has_side_effects=True),
        name="gradient_and_combine",
    )(offsets[0], pos_counts, grouped(amplitude), grouped(phase_map), probe_modes, measured[0], jnp.asarray(tables), jnp.asarray(kernel))
    return updated.reshape(1, 2, LAYERS, TILE, TILE)


def solution(mesh):
    in_specs = (
        P("tile", None, None, None),
        P("tile", None, None, None),
        P(),
        P("tile", "pos", None),
        P("tile", "pos"),
        P("tile", "pos", None, None),
    )
    out_specs = P("tile", None, None, None, None)
    return jax.shard_map(per_device, mesh=mesh, in_specs=in_specs, out_specs=out_specs, check_vma=False)
```

```python
import functools
import math

import jax
import jax.numpy as jnp
import numpy as np
from jax import lax
from jax.experimental import pallas as pl
from jax.experimental.pallas import tpu as pltpu
from jax.sharding import PartitionSpec as P

MESH = pl.DeviceIdType.MESH
TILE = 256
WIN = 128
EDGE = 64
MODES = 3
LAYERS = 2
SLOTS = 2
SPAN = WIN + 8
LEAD = (TILE - SPAN) // 8
SUBS = 2
HIGH = 16 // SUBS
CHUNKS = LAYERS * SUBS
STEP = 0.1
FRESNEL = 0.0123
SIN = (0.9999999957326958, -0.16666657991741893, 0.008333051059307331, -0.0001980907498047039, 2.605224199925007e-06)
COS = (0.9999999997806426, -0.49999999358456015, 0.04166663625748454, -0.001388836139270363, 2.476016095941152e-05, -2.6051488147238807e-07)


def make_tables():
    counter = np.arange(WIN)
    angles = (np.outer(counter, counter) % WIN).astype(np.float32) * np.float32(2.0 * math.pi / WIN)
    scaling = np.float32(1.0 / math.sqrt(WIN))
    f_re = (np.cos(angles) * scaling).astype(jnp.bfloat16)
    f_im = (-np.sin(angles) * scaling).astype(jnp.bfloat16)
    forward = np.block([[f_re, f_im], [-f_im, f_re]])
    inverse = np.block([[f_re, -f_im], [f_im, f_re]])
    centered = ((counter + WIN // 2) % WIN - WIN // 2).astype(np.float32)
    square = centered * centered
    phases = np.float32(-FRESNEL) * (square[:, None] + square[None, :])
    kernel = np.stack([np.cos(phases), np.sin(phases)]).astype(np.float32)
    return np.stack([forward, inverse]).astype(jnp.bfloat16), kernel


def horner(terms, u):
    total = jnp.full_like(u, terms[-1])
    for term in terms[-2::-1]:
        total = total * u + term
    return total


def polar(amplitude, phase):
    half = phase * 0.5
    u = half * half
    sine = half * horner(SIN, u)
    cosine = horner(COS, u)
    return amplitude - (2.0 * amplitude) * (sine * sine), (2.0 * amplitude) * (sine * cosine)


def times(a, b):
    return a[0] * b[0] - a[1] * b[1], a[0] * b[1] + a[1] * b[0]


def times_conj(a, b):
    return a[0] * b[0] + a[1] * b[1], a[1] * b[0] - a[0] * b[1]


def right_pass(waves, table):
    rows = [jnp.concatenate([re.astype(jnp.bfloat16), im.astype(jnp.bfloat16)], axis=1) for re, im in waves]
    result = jnp.dot(jnp.concatenate(rows, axis=0), table, preferred_element_type=jnp.float32)
    return [(result[i * WIN : (i + 1) * WIN, :WIN], result[i * WIN : (i + 1) * WIN, WIN:]) for i in range(len(waves))]


def left_pass(waves, table):
    columns = [jnp.concatenate([re.astype(jnp.bfloat16), im.astype(jnp.bfloat16)], axis=0) for re, im in waves]
    result = jnp.dot(table, jnp.concatenate(columns, axis=1), preferred_element_type=jnp.float32)
    return [(result[:WIN, i * WIN : (i + 1) * WIN], result[WIN:, i * WIN : (i + 1) * WIN]) for i in range(len(waves))]


def transform(waves, right, left):
    return left_pass(right_pass(waves, right), left)


def transform_back(waves, right, left):
    return right_pass(left_pass(waves, left), right)


def crop(ref, layer, group, shift, column):
    lane = lax.broadcasted_iota(jnp.int32, (8, WIN), 1)
    sublane = lax.broadcasted_iota(jnp.int32, (8, WIN), 0)
    rows = []
    for j in range(SPAN // 8):
        row = ref[layer, group + j]
        rows.append(pltpu.roll(jnp.where(lane >= column, row[:, :WIN], row[:, WIN:]), (WIN - column) & (WIN - 1), 1))
    picked = [
        pltpu.roll(jnp.where(sublane >= shift, rows[j], rows[j + 1]), (8 - shift) & 7, 0) for j in range(WIN // 8)
    ]
    return jnp.concatenate(picked, axis=0)


def add_all(values):
    total = values[0]
    for value in values[1:]:
        total = total + value
    return total


def spread_out(value, shift, column):
    lane = lax.broadcasted_iota(jnp.int32, (8, WIN), 1)
    sublane = lax.broadcasted_iota(jnp.int32, (8, WIN), 0)
    zero = jnp.zeros((8, WIN), jnp.float32)
    turned = [pltpu.roll(value[8 * j : 8 * j + 8], shift & 7, 0) for j in range(WIN // 8)]
    placed = []
    for j in range(SPAN // 8):
        before = turned[j - 1] if j else zero
        after = turned[j] if j < WIN // 8 else zero
        row = pltpu.roll(jnp.where(sublane >= shift, after, before), column & (WIN - 1), 1)
        placed.append(jnp.concatenate([jnp.where(lane >= column, row, 0.0), jnp.where(lane >= column, 0.0, row)], axis=1))
    return placed


def sum_modes(pairs):
    return add_all([v[0] for v in pairs]), add_all([v[1] for v in pairs])


def fused_kernel(
    off_ref, count_ref, amp_hbm, phase_hbm, probe_hbm, measured_hbm, tables_hbm, kernel_hbm, out_ref,
    amp_ref, phase_ref, probe_ref, measured_ref, tables_ref, kernel_ref, load_sem, pad, grad, pair, half, xin, block, zin, total, strips, strips_in, rows_in, send, recv,
):
    places = (
        (amp_hbm, amp_ref), (phase_hbm, phase_ref), (probe_hbm, probe_ref), (tables_hbm, tables_ref),
        (kernel_hbm, kernel_ref), (measured_hbm, measured_ref),
    )
    loads = [pltpu.make_async_copy(src, dst, load_sem.at[i]) for i, (src, dst) in enumerate(places)]
    for load in loads:
        load.start()
    tile, pos = lax.axis_index("tile"), lax.axis_index("pos")
    tiles = lax.axis_size("tile")
    core, z_hi, x = lax.rem(pos, 2), lax.rem(pos // 2, 2), pos // 4
    z_lo = lax.rem(tile, 4)
    xs = [lax.rem(x + step, 4) for step in range(4)]

    def at(tile_step, x_, z_, core_):
        return {"tile": lax.rem(tile + tiles + tile_step, tiles), "pos": x_ * 4 + z_ * 2 + core_}

    sibling = at(0, x, z_hi, 1 - core)
    along_x = {step: at(0, xs[step], z_hi, core) for step in (1, 2, 3)}
    crossed = {step: at(0, xs[step], z_hi, 1 - core) for step in (1, 2, 3)}
    across = at(0, x, 1 - z_hi, core)
    after = at(1, x, jnp.where(z_lo == 3, 1 - z_hi, z_hi), core)
    before = at(-1, x, jnp.where(z_lo == 0, 1 - z_hi, z_hi), core)
    below = at(4, x, z_hi, core)
    above = at(-4, x, z_hi, core)

    partners = (sibling, along_x[1], along_x[3], along_x[2], across, after, before, below, above) + tuple(crossed.values())
    barrier = pltpu.get_barrier_semaphore()
    for partner in partners:
        pl.semaphore_signal(barrier, inc=1, device_id=partner, device_id_type=MESH)

    started = []

    def push(chunk, index, src, dst, device):
        copy = pltpu.make_async_remote_copy(
            src_ref=src, dst_ref=dst, send_sem=send.at[chunk, index], recv_sem=recv.at[chunk, index],
            device_id=device, device_id_type=MESH,
        )
        copy.start()
        started.append(copy)
        return copy

    def rows_of(x_, core_, sub):
        return pl.ds(pl.multiple_of(lax.rem(x_, 2) * 32 + core_ * 16 + sub * HIGH, HIGH), HIGH)

    def flat(value):
        return value.reshape(4 * HIGH, TILE)

    slots = range(SLOTS)
    groups, shifts, columns = [], [], []
    lives = [(count_ref[0, 0] - slot).astype(jnp.float32) for slot in slots]
    lives = [jnp.clip(jnp.full((1, WIN), live), 0.0, 1.0) for live in lives]
    for slot in slots:
        row = off_ref[slot, 0]
        group = lax.shift_right_logical(row - lax.shift_right_logical(row, 7), 3)
        groups.append(group)
        shifts.append(row - group * 8)
        columns.append(off_ref[slot, 1])

    def kernel():
        return kernel_ref[0], kernel_ref[1]

    def probe(m):
        return probe_ref[0, m], probe_ref[1, m]

    def deposit(slot, layer, grads):
        for part in range(2):
            value = grads[part] * lives[slot]
            for j, row in enumerate(spread_out(value, shifts[slot], columns[slot])):
                pad[slot, part, layer, LEAD + j] = row

    def collect(layer):
        for part in range(2):
            for r in range(TILE // 8):
                first, second = [pad[slot, part, layer, LEAD - groups[slot] + r] for slot in slots]
                grad[layer, part, r // 8, r % 8 * 8 : r % 8 * 8 + 8, :] = first + second

    empty = jnp.zeros((LEAD, 8, TILE), jnp.float32)
    for slot in slots:
        for part in range(2):
            for layer in range(LAYERS):
                pad[slot, part, layer, 0:LEAD] = empty
                pad[slot, part, layer, LEAD + SPAN // 8 :] = empty

    def each(stage, *lists):
        return [stage(*items) for items in zip(*lists)]

    modes = range(MODES)
    def crop_layer(layer):
        return [
            polar(
                crop(amp_ref, layer, groups[slot], shifts[slot], columns[slot]),
                crop(phase_ref, layer, groups[slot], shifts[slot], columns[slot]),
            )
            for slot in slots
        ]

    loads[0].wait()
    loads[1].wait()
    layers = [crop_layer(layer) for layer in range(LAYERS)]
    for load in loads[2:]:
        load.wait()
    forward, inverse = tables_ref[0], tables_ref[1]
    waves = [[times(probe(m), layers[0][slot]) for m in modes] for slot in slots]
    layers = list(zip(*layers))
    waves = each(lambda w: right_pass(w, forward), waves)
    waves = each(lambda w: left_pass(w, inverse), waves)
    waves = each(lambda w: [times(v, kernel()) for v in w], waves)
    waves = each(lambda w: right_pass(w, inverse), waves)
    returned = each(lambda w: left_pass(w, forward), waves)
    waves = each(lambda w, o: [times(v, o[1]) for v in w], returned, layers)
    waves = each(lambda w: right_pass(w, forward), waves)
    far = each(lambda w: left_pass(w, inverse), waves)

    def pull(slot, w):
        misfit = add_all([re * re + im * im for re, im in w]) - measured_ref[slot]
        twice = misfit + misfit
        return [(twice * re, twice * im) for re, im in w]

    waves = each(pull, slots, far)
    waves = each(lambda w: left_pass(w, forward), waves)
    waves = each(lambda w: right_pass(w, inverse), waves)
    for slot in slots:
        deposit(slot, 1, sum_modes([times_conj(g, r) for g, r in zip(waves[slot], returned[slot])]))
    collect(1)

    def swap_pair(chunk):
        layer, sub = divmod(chunk, SUBS)
        copies = []
        for step in (2, 1, 3, 0):
            owner = xs[step]
            src = grad.at[layer, owner // 2, :, rows_of(owner, 1 - core, sub)]
            copies.append((step, push(chunk, step, src, pair.at[chunk, step], sibling)))
        return copies

    def spread_x(chunk, swaps):
        layer, sub = divmod(chunk, SUBS)
        copies = []
        for step, swap in swaps:
            swap.wait_recv()
            owner = xs[step]
            half[chunk, step] = grad[layer, owner // 2, :, rows_of(owner, core, sub), :] + pair[chunk, step]
            if step:
                copies.append(push(chunk, 3 + step, half.at[chunk, step], xin.at[chunk, step - 1], along_x[step]))
        return copies

    def swap_z(chunk, copies):
        for copy in copies:
            copy.wait_recv()
        block[chunk] = half[chunk, 0] + (xin[chunk, 0] + xin[chunk, 2] + xin[chunk, 1])
        return push(chunk, 7, block.at[chunk], zin.at[chunk], across)

    low = lax.broadcasted_iota(jnp.int32, (2 * HIGH, WIN), 1) < EDGE

    def swap_strips(chunk, copy):
        copy.wait_recv()
        total[chunk] = block[chunk] + zin[chunk]
        copies = [
            push(chunk, 8, total.at[chunk, 3], rows_in.at[chunk, 0], below),
            push(chunk, 9, total.at[chunk, 0], rows_in.at[chunk, 1], above),
        ]
        value = flat(total[chunk])
        left, right = value[:, :WIN], value[:, WIN:]
        strips[chunk, 0] = jnp.where(low, pltpu.roll(right[: 2 * HIGH], EDGE, 1), right[2 * HIGH :])
        strips[chunk, 1] = jnp.where(low, left[: 2 * HIGH], pltpu.roll(left[2 * HIGH :], EDGE, 1))
        copies.append(push(chunk, 10, strips.at[chunk, 0], strips_in.at[chunk, 0], after))
        copies.append(push(chunk, 11, strips.at[chunk, 1], strips_in.at[chunk, 1], before))
        return copies

    def share(chunk, index, step, device):
        layer, sub = divmod(chunk, SUBS)
        owner = xs[step]
        view = out_ref.at[owner // 2, layer, :, rows_of(owner, core, sub)]
        return push(chunk, index, view, view, device)

    def object_block(chunk):
        layer, sub = divmod(chunk, SUBS)
        first = lax.rem(x, 2) * 4 + core * 2 + sub * (HIGH // 8)

        def read(ref):
            return jnp.concatenate(
                [ref[layer, pl.ds(p * 8 + first, HIGH // 8)].reshape(HIGH, TILE) for p in range(4)], axis=0
            )

        both = polar(read(amp_ref), read(phase_ref))
        return jnp.where(x < 2, both[0], both[1])

    def update(chunk, copies, base):
        layer, sub = divmod(chunk, SUBS)
        for copy in copies:
            copy.wait_recv()
        from_left = jnp.where(tile > 0, strips_in[chunk, 0], 0.0)
        from_right = jnp.where(tile < tiles - 1, strips_in[chunk, 1], 0.0)
        left = jnp.concatenate(
            [jnp.where(low, from_left, 0.0), jnp.where(low, pltpu.roll(from_left, EDGE, 1), 0.0)], axis=0
        )
        right = jnp.concatenate(
            [jnp.where(low, 0.0, pltpu.roll(from_right, EDGE, 1)), jnp.where(low, 0.0, from_right)], axis=0
        )
        top = jnp.where(tile >= 4, rows_in[chunk, 0], 0.0)
        bottom = jnp.where(tile < tiles - 4, rows_in[chunk, 1], 0.0)
        ends = jnp.concatenate([top, jnp.zeros((2 * HIGH, TILE), jnp.float32), bottom], axis=0)
        combined = flat(total[chunk]) + jnp.concatenate([left, right], axis=1) + ends
        out_ref[x // 2, layer, :, rows_of(x, core, sub), :] = (base - STEP * combined).reshape(4, HIGH, TILE)
        remote = [(step, share(chunk, 11 + step, 0, along_x[step])) for step in (2, 1, 3)]
        local = [share(chunk, 15, 0, sibling)]
        if chunk == SUBS - 1:
            local += [share(chunk, 15 + step, 0, crossed[step]) for step in (2, 1, 3)]
        return remote, local

    def relay(chunk, remote, local):
        for step, copy in remote:
            copy.wait_recv()
            if chunk == SUBS - 1:
                continue
            local.append(share(chunk, 15 + step, 4 - step, sibling))
        return local

    late = list(range(SUBS, CHUNKS))
    early = list(range(SUBS))
    order = late + early
    pl.semaphore_wait(barrier, len(partners))
    swaps = {chunk: swap_pair(chunk) for chunk in late}
    waves = each(lambda w, o: [times_conj(v, o[1]) for v in w], waves, layers)
    waves = each(lambda w: left_pass(w, inverse), waves)
    waves = each(lambda w: right_pass(w, forward), waves)
    waves = each(lambda w: [times_conj(v, kernel()) for v in w], waves)
    waves = each(lambda w: left_pass(w, forward), waves)
    waves = each(lambda w: right_pass(w, inverse), waves)
    sums = {chunk: spread_x(chunk, swaps[chunk]) for chunk in late}
    for slot in slots:
        deposit(slot, 0, sum_modes([times_conj(waves[slot][m], probe(m)) for m in modes]))
    collect(0)
    swaps.update({chunk: swap_pair(chunk) for chunk in early})
    bases = {chunk: object_block(chunk) for chunk in order}
    for chunk in early:
        sums[chunk] = spread_x(chunk, swaps[chunk])
    blocks = {chunk: swap_z(chunk, sums[chunk]) for chunk in order}
    edges = {chunk: swap_strips(chunk, blocks[chunk]) for chunk in order}
    shares = {chunk: update(chunk, edges[chunk], bases[chunk]) for chunk in order}
    ends = [relay(chunk, *shares[chunk]) for chunk in order]
    for local in ends:
        for copy in local:
            copy.wait_recv()
    for copy in started:
        copy.wait_send()


def grouped(tile_array):
    return tile_array.reshape(LAYERS, TILE // 8, 8, TILE)


def per_device(amplitude, phase_map, probe_modes, offsets, pos_counts, measured):
    tables, kernel = make_tables()
    vmem = pl.BlockSpec(memory_space=pltpu.VMEM)
    smem = pl.BlockSpec(memory_space=pltpu.SMEM)
    f32 = jnp.float32
    updated = pl.pallas_call(
        fused_kernel,
        out_shape=pltpu.VMEM((2, LAYERS, 4, EDGE, TILE), f32),
        in_specs=[smem, smem] + [pl.BlockSpec(memory_space=pl.ANY)] * 6,
        out_specs=vmem,
        scratch_shapes=[
            pltpu.VMEM((LAYERS, TILE // 8, 8, TILE), f32),
            pltpu.VMEM((LAYERS, TILE // 8, 8, TILE), f32),
            pltpu.VMEM((2, MODES, WIN, WIN), f32),
            pltpu.VMEM((SLOTS, WIN, WIN), f32),
            pltpu.VMEM((2, TILE, TILE), jnp.bfloat16),
            pltpu.VMEM((2, WIN, WIN), f32),
            pltpu.SemaphoreType.DMA((6,)),
            pltpu.VMEM((SLOTS, 2, LAYERS, 2 * LEAD + SPAN // 8, 8, TILE), f32),
            pltpu.VMEM((LAYERS, 2, 4, EDGE, TILE), f32),
            pltpu.VMEM((CHUNKS, 4, 4, HIGH, TILE), f32),
            pltpu.VMEM((CHUNKS, 4, 4, HIGH, TILE), f32),
            pltpu.VMEM((CHUNKS, 3, 4, HIGH, TILE), f32),
            pltpu.VMEM((CHUNKS, 4, HIGH, TILE), f32),
            pltpu.VMEM((CHUNKS, 4, HIGH, TILE), f32),
            pltpu.VMEM((CHUNKS, 4, HIGH, TILE), f32),
            pltpu.VMEM((CHUNKS, 2, 2 * HIGH, WIN), f32),
            pltpu.VMEM((CHUNKS, 2, 2 * HIGH, WIN), f32),
            pltpu.VMEM((CHUNKS, 2, HIGH, TILE), f32),
            pltpu.SemaphoreType.DMA((CHUNKS, 19)),
            pltpu.SemaphoreType.DMA((CHUNKS, 19)),
        ],
        compiler_params=pltpu.CompilerParams(collective_id=0, has_side_effects=True),
        name="gradient_and_combine",
    )(offsets[0], pos_counts, grouped(amplitude), grouped(phase_map), probe_modes, measured[0], jnp.asarray(tables), jnp.asarray(kernel))
    return updated.reshape(1, 2, LAYERS, TILE, TILE)


def solution(mesh):
    in_specs = (
        P("tile", None, None, None),
        P("tile", None, None, None),
        P(),
        P("tile", "pos", None),
        P("tile", "pos"),
        P("tile", "pos", None, None),
    )
    out_specs = P("tile", None, None, None, None)
    return jax.shard_map(per_device, mesh=mesh, in_specs=in_specs, out_specs=out_specs, check_vma=False)
```
